256 devices in a mesh: narrow: 8 (over x, z_lo), wide: 32 (over y, z_hi, core).
Axes of the slice: x: 4, y: 4, z: 8 (z_hi: 4, z_lo: 2; z = z_hi * 2 + z_lo), core: 2. Of those that a mesh axis runs over, the one named last changes fastest.
Arguments:
- basis: bfloat16 [128, 32, 512, 128], P(None, 'narrow', 'wide'), may hold values from -6 to 6
- rhs: bfloat16 [32, 512, 128], P('narrow', 'wide'), may hold values from -48 to 48
- coeffs: float32 [4, 32, 512, 128], P(None, 'narrow', 'wide'), may hold values from 0.25 to 4
- rows: int32 [4, 32, 512, 128], P(None, 'narrow', 'wide'), may hold values from 0 to 255
- signs: int32 [4, 32, 512, 128], P(None, 'narrow', 'wide'), may hold values from 0 to 1
- params: float32 [256, 4], P(('narrow', 'wide')), may hold values from 0.25 to 4
- order: int32 [256], replicated, may hold values from 0 to 255, each once
Outputs:
- fields: bfloat16 [256, 32, 512, 128], P(None, 'narrow', 'wide')
The draws below stay inside these ranges and needn't reach their ends.
Inputs may be any that keep to these rules, and one draw needn't show every extreme that they name: `order`: each point number appears exactly once.
All inputs are finite; a program needn't handle non-finite values.
Results may differ from the reference program's by a relative error of at most 0.0056.
Values may be sent and summed in bfloat16 or wider, within the bound.
No kernel may reach another device: no remote copies, remote signals or barrier semaphores. Data moves between devices by JAX's collectives and lax.ppermute only.
A program may use at most 64 MiB of HBM per device.

```python
import math
import jax
import jax.numpy as jnp
from jax import lax

K = 128
M = 1024
TERMS = 4
NNZ = 4
NX = 32
NY = 512
NZ = 128
P_SIZE = 256
R = 256


def touch_ends(result, own_key, smallest, top_value):
    place = [jax.random.randint(jax.random.fold_in(own_key, axis), (), 0, length) for axis, length in enumerate(result.shape)]
    main_axis = result.shape.index(max(result.shape))
    beside = place[:main_axis] + [(place[main_axis] + 1) % result.shape[main_axis]] + place[main_axis + 1:]
    return result.at[tuple(place)].set(smallest).at[tuple(beside)].set(top_value)


def level_of(stream_key, dims, shards, smallest, top_value):
    def one(dim, blocks):
        draws = jax.random.uniform(jax.random.fold_in(jax.random.fold_in(stream_key, 6), dim), (blocks,), jnp.float32, smallest / len(shards), top_value / len(shards))
        return jnp.repeat(jnp.exp(draws), dims[dim] // blocks).reshape((-1,) + (1,) * (len(dims) - dim - 1))

    level = one(*shards[0])
    for cut in shards[1:]:
        level = level * one(*cut)
    return level


def scatter_about(key, shape, width, most, pieces=(), kind=jnp.bfloat16):
    values = jax.random.normal(key, shape, jnp.float32) * width
    if len(pieces) > 0:
        values = level_of(key, shape, pieces, -0.22, 0.18) * values
    return jnp.clip(values, min=-most, max=most).astype(kind)


def setup_inputs(seed: int = 0) -> dict:
    arg_keys = jax.random.split(jax.random.key(seed), 8)
    return {
        "basis": scatter_about(arg_keys[0], (K, NX, NY, NZ), 1.0, 6.0, ((1, 8), (2, 32))),
        "rhs": scatter_about(arg_keys[1], (NX, NY, NZ), 8.0, 48.0, ((0, 8), (1, 32))),
        "coeffs": jnp.clip(jnp.exp(math.log(4.0) - 2.7725887 * jax.random.uniform(arg_keys[2], (TERMS, NX, NY, NZ), jnp.float32) ** level_of(arg_keys[2], (TERMS, NX, NY, NZ), ((1, 8), (2, 32)), -0.2, 0.2)), 0.25, 4.0),
        "rows": touch_ends(jax.random.randint(arg_keys[3], (NNZ, NX, NY, NZ), 0, R), jax.random.fold_in(arg_keys[3], 1), 0, R - 1).astype(jnp.int32),
        "signs": touch_ends(jax.random.randint(arg_keys[4], (NNZ, NX, NY, NZ), 0, 2), jax.random.fold_in(arg_keys[4], 1), 0, 1).astype(jnp.int32),
        "params": jnp.clip(jnp.exp(math.log(4.0) - 2.7725887 * jax.random.uniform(arg_keys[5], (P_SIZE, TERMS), jnp.float32) ** level_of(arg_keys[5], (P_SIZE, TERMS), ((0, 256),), -0.2, 0.2)), 0.25, 4.0),
        "order": jax.random.permutation(arg_keys[6], P_SIZE).astype(jnp.int32),
    }


def reference(basis, rhs, coeffs, rows, signs, params, order):
    row_block = M // NNZ
    padded = jnp.pad(basis, ((0, 0), (1, 1), (1, 1), (1, 1)))
    offsets = lax.broadcasted_iota(jnp.int32, (NNZ, 1), 0) * row_block

    def slab(carry, index):
        sketch_sum, rhs_sum = carry
        window = lax.dynamic_slice_in_dim(padded, index, 3, 1).astype(jnp.float32)
        centre = window[:, 1, 1:-1, 1:-1]
        along_x = 2.0 * centre - window[:, 0, 1:-1, 1:-1] - window[:, 2, 1:-1, 1:-1]
        along_y = 2.0 * centre - window[:, 1, :-2, 1:-1] - window[:, 1, 2:, 1:-1]
        along_z = 2.0 * centre - window[:, 1, 1:-1, :-2] - window[:, 1, 1:-1, 2:]
        local_coef = lax.dynamic_index_in_dim(coeffs, index, 1, keepdims=False)
        terms = jnp.stack([local_coef[0] * centre, local_coef[1] * along_x, local_coef[2] * along_y, local_coef[3] * along_z])
        terms = terms.astype(jnp.bfloat16).reshape(TERMS * K, NY * NZ).astype(jnp.float32)
        hashed = lax.dynamic_index_in_dim(rows, index, 1, keepdims=False).reshape(NNZ, NY * NZ)
        targets = (hashed + offsets).reshape(-1)
        sign_raw = lax.dynamic_index_in_dim(signs, index, 1, keepdims=False).reshape(NNZ, NY * NZ)
        sign_values = (2 * sign_raw - 1).astype(jnp.float32) * 0.5
        scaled = sign_values[:, :, None] * jnp.transpose(terms)[None, :, :]
        sketch_sum = sketch_sum + jax.ops.segment_sum(scaled.reshape(-1, TERMS * K), targets, num_segments=M)
        source = lax.dynamic_index_in_dim(rhs, index, 0, keepdims=False).astype(jnp.float32).reshape(1, NY * NZ)
        rhs_sum = rhs_sum + jax.ops.segment_sum((sign_values * source).reshape(-1), targets, num_segments=M)
        return ((sketch_sum, rhs_sum), None)
    start = (jnp.zeros((M, TERMS * K), jnp.float32), jnp.zeros((M,), jnp.float32))
    (sketched, sketched_rhs), _ = lax.scan(slab, start, jnp.arange(NX, dtype=jnp.int32))
    gram = jnp.dot(sketched.T, sketched, precision=lax.Precision.HIGHEST)
    projected = jnp.dot(sketched.T, sketched_rhs, precision=lax.Precision.HIGHEST)
    gram_blocks = gram.reshape(TERMS, K, TERMS, K)
    proj_blocks = projected.reshape(TERMS, K)
    pair_weight = params[:, :, None] * params[:, None, :]
    normal = jnp.einsum('pqr,qirj->pij', pair_weight, gram_blocks, precision=lax.Precision.HIGHEST)
    right_side = jnp.einsum('pq,qi->pi', params, proj_blocks, precision=lax.Precision.HIGHEST)
    coefficients = jnp.linalg.solve(normal, right_side[:, :, None])[:, :, 0].astype(jnp.bfloat16)
    picked = coefficients[order]
    fields = jnp.dot(picked.astype(jnp.float32), basis.reshape(K, -1).astype(jnp.float32), preferred_element_type=jnp.float32)
    return fields.astype(jnp.bfloat16).reshape(P_SIZE, NX, NY, NZ)
```

```python
import jax
import jax.numpy as jnp
from jax import lax
from jax.experimental import pallas as pl
from jax.experimental.pallas import tpu as pltpu
from jax.sharding import Mesh
from jax.sharding import PartitionSpec as P

K = 128
M = 1024
TERMS = 4
NNZ = 4
ROWS = M // NNZ
NX = 4
NY = 16
NZ = 128
CELLS = NY * NZ
TALL = TERMS * K + 16
CHIPS = 128
CHUNK = 24
POINTS = 256
TOL2 = 1e-10
MAX_ROUNDS = 256

f32 = jnp.float32
bf16 = jnp.bfloat16


def put_hash(hash_ref, lane, row_of, sign_of):
    slots = lax.broadcasted_iota(jnp.int32, (ROWS, NZ), 0)
    for j in range(NNZ):
        chosen = jnp.where(slots == row_of(j), sign_of(j), 0.0)
        hash_ref[j * ROWS:(j + 1) * ROWS, pl.ds(lane, NZ)] = chosen.astype(bf16)


def nt(a, b):
    return lax.dot_general(a, b, (((1,), (1,)), ((), ())), preferred_element_type=f32)


def in_two(source):
    high = source.astype(bf16).astype(f32)
    return (high + pltpu.roll(source - high, 2, 0)).astype(bf16)


def sketch_body(basis_ref, rhs_ref, co_ref, rows_ref, signs_ref, acc_ref, bt_ref, flat, pad, terms, hashes, source_ref):
    def widen(i, _):
        k = pl.multiple_of(i * 8, 8)
        flat[pl.ds(pl.multiple_of(k * NX * NY, 512), 512), :] = (
            basis_ref[pl.ds(k, 8)].astype(f32).reshape(8 * NX * NY, NZ)
        )
        return 0

    lax.fori_loop(0, K // 8, widen, 0)
    pad[0] = jnp.zeros((K, (NY + 2) * NZ), f32)
    pad[NX + 1] = jnp.zeros((K, (NY + 2) * NZ), f32)
    for x in range(NX):
        pad[x + 1, :, 0:NZ] = jnp.zeros((K, NZ), f32)
        pad[x + 1, :, (NY + 1) * NZ:] = jnp.zeros((K, NZ), f32)

    def turn(i, _):
        x = i // NY
        y = i % NY
        tile = flat[pl.ds(i, K, stride=NX * NY), :]
        pad[x + 1, :, pl.ds(pl.multiple_of((y + 1) * NZ, NZ), NZ)] = tile
        bt_ref[x, :, pl.ds(pl.multiple_of(y * NZ, NZ), NZ)] = tile.astype(bf16)
        return 0

    lax.fori_loop(0, NX * NY, turn, 0)
    lane = lax.broadcasted_iota(jnp.int32, (K, NZ), 1)

    def plane(x, _):
        source_ref[...] = rhs_ref[x].astype(f32)

        def group(y, _):
            here = pl.multiple_of(y * NZ, NZ)
            above = pl.multiple_of(y * NZ + NZ, NZ)
            v = pad[x + 1, :, pl.ds(above, NZ)]
            v2 = v + v
            along_x = v2 - pad[x, :, pl.ds(above, NZ)] - pad[x + 2, :, pl.ds(above, NZ)]
            along_y = v2 - pad[x + 1, :, pl.ds(here, NZ)] - pad[x + 1, :, pl.ds(pl.multiple_of(y * NZ + 2 * NZ, NZ), NZ)]
            lower = jnp.where(lane == 0, 0.0, pltpu.roll(v, 1, 1))
            upper = jnp.where(lane == NZ - 1, 0.0, pltpu.roll(v, NZ - 1, 1))
            along_z = v2 - lower - upper
            for q, t in enumerate((v, along_x, along_y, along_z)):
                terms[q * K:(q + 1) * K, pl.ds(here, NZ)] = (co_ref[q, x, pl.ds(y, 1), :] * t).astype(bf16)
            source = source_ref[pl.ds(y, 1), :]
            top = lax.broadcasted_iota(jnp.int32, (16, NZ), 0) == 0
            terms[TERMS * K:TALL, pl.ds(here, NZ)] = jnp.where(top, source, 0.0).astype(bf16)
            put_hash(
                hashes,
                here,
                lambda j: rows_ref[j, x, pl.ds(y, 1), :],
                lambda j: signs_ref[j, x, pl.ds(y, 1), :].astype(f32) - 0.5,
            )
            return 0

        lax.fori_loop(0, NY, group, 0)
        got = nt(terms[...], hashes[...])

        @pl.when(x == 0)
        def _():
            acc_ref[...] = got

        @pl.when(x > 0)
        def _():
            acc_ref[...] += got

        return 0

    lax.fori_loop(0, NX, plane, 0)


def sketch(basis, rhs, coeffs, rows, signs):
    return pl.pallas_call(
        sketch_body,
        out_shape=(
            jax.ShapeDtypeStruct((TALL, M), f32),
            jax.ShapeDtypeStruct((NX, K, CELLS), bf16),
        ),
        scratch_shapes=[
            pltpu.VMEM((K * NX * NY, NZ), f32),
            pltpu.VMEM((NX + 2, K, (NY + 2) * NZ), f32),
            pltpu.VMEM((TALL, CELLS), bf16),
            pltpu.VMEM((M, CELLS), bf16),
            pltpu.VMEM((NY, NZ), f32),
        ],
        compiler_params=pltpu.CompilerParams(vmem_limit_bytes=56 << 20),
        name="sketch",
    )(basis, rhs, coeffs, rows, signs)


def edge_body(core_ref, acc_in, bt_ref, xl_ref, xu_ref, yl_ref, yu_ref, own_ref, other_ref, acc, terms, hashes):
    acc[...] = acc_in[...]

    def one(info, plane_x, lane_in, y_info, place):
        v = bt_ref[plane_x, :, pl.ds(lane_in, NZ)].astype(f32)
        terms[:, pl.ds(place, NZ)] = (-info[2 * NNZ, pl.ds(y_info, 1), :] * v).astype(bf16)
        put_hash(
            hashes,
            place,
            lambda j: info[j, pl.ds(y_info, 1), :].astype(jnp.int32),
            lambda j: info[NNZ + j, pl.ds(y_info, 1), :] - 0.5,
        )

    for info, plane_x in ((xl_ref, 0), (xu_ref, NX - 1)):
        def group(y, _):
            here = pl.multiple_of(y * NZ, NZ)
            one(info, plane_x, here, y, here)
            return 0

        lax.fori_loop(0, NY, group, 0)
        acc[K:2 * K, :] += nt(terms[...], hashes[...])
    for x in range(NX):
        one(yl_ref, x, 0, x, x * NZ)
        one(yu_ref, x, (NY - 1) * NZ, x, (NX + x) * NZ)
    acc[2 * K:3 * K, :] += nt(terms[:, :2 * NX * NZ], hashes[:, :2 * NX * NZ])

    c = core_ref[0]
    row = lax.broadcasted_iota(jnp.int32, (8, NZ), 0)

    def split(g, _):
        mine = pl.multiple_of(c * 2 * K + g * 16, 16)
        theirs = pl.multiple_of((1 - c) * 2 * K + g * 16, 16)
        for l in range(M // NZ):
            own_ref[g * 8 + l, 0:16, :] = acc[pl.ds(mine, 16), l * NZ:(l + 1) * NZ]
            other_ref[g * 8 + l, 0:16, :] = acc[pl.ds(theirs, 16), l * NZ:(l + 1) * NZ].astype(bf16)
            own_ref[g * 8 + l, 16:24, :] = jnp.zeros((8, NZ), f32)
            other_ref[g * 8 + l, 16:24, :] = jnp.zeros((8, NZ), bf16)
        return 0

    lax.fori_loop(0, 2 * K // 16, split, 0)
    for l in range(M // NZ):
        source = jnp.where(row == 0, acc[TERMS * K:TERMS * K + 8, l * NZ:(l + 1) * NZ], 0.0)
        own_ref[l, 16:24, :] = source
        other_ref[l, 16:24, :] = in_two(source)


def edges(core, acc, bt, infos):
    vm = pl.BlockSpec(memory_space=pltpu.VMEM)
    return pl.pallas_call(
        edge_body,
        in_specs=[pl.BlockSpec(memory_space=pltpu.SMEM)] + [vm] * 6,
        out_shape=(
            jax.ShapeDtypeStruct((CHIPS, CHUNK, NZ), f32),
            jax.ShapeDtypeStruct((CHIPS, CHUNK, NZ), bf16),
        ),
        scratch_shapes=[
            pltpu.VMEM((TALL, M), f32),
            pltpu.VMEM((K, CELLS), bf16),
            pltpu.VMEM((M, CELLS), bf16),
        ],
        compiler_params=pltpu.CompilerParams(vmem_limit_bytes=56 << 20),
        name="edges",
    )(core, acc, bt, *infos)


def merge_body(own_ref, got_ref, out_ref):
    def add(i, _):
        at = pl.ds(pl.multiple_of(i * 8, 8), 8)
        out_ref[at, 0:16, :] = (own_ref[at, 0:16, :] + got_ref[at, 0:16, :].astype(f32)).astype(bf16)
        out_ref[at, 16:24, :] = jnp.zeros((8, 8, NZ), bf16)
        return 0

    lax.fori_loop(0, CHIPS // 8, add, 0)
    row = lax.broadcasted_iota(jnp.int32, (8, NZ), 0)
    for l in range(M // NZ):
        got = got_ref[l, 16:24, :].astype(f32)
        source = own_ref[l, 16:24, :] + (got + pltpu.roll(got, 6, 0))
        out_ref[l, 16:24, :] = in_two(jnp.where(row == 0, source, 0.0))


def merge(own, got):
    return pl.pallas_call(
        merge_body,
        out_shape=jax.ShapeDtypeStruct((CHIPS, CHUNK, NZ), bf16),
        name="merge",
    )(own, got)


def total_body(params_ref, parts_ref, out_ref):
    def add(i, carry):
        a, b = carry
        m = i * 8
        for s in range(8):
            a = a + parts_ref[m + s, 0:16, :].astype(f32)
            b = b + parts_ref[m + s, 16:24, :].astype(f32)
        return (a, b)

    a, b = lax.fori_loop(0, CHIPS // 8, add, (jnp.zeros((16, NZ), f32), jnp.zeros((8, NZ), f32)))
    lane = lax.broadcasted_iota(jnp.int32, (8, NZ), 1)
    row = lax.broadcasted_iota(jnp.int32, (8, NZ), 0)
    weights = jnp.zeros((8, NZ), f32)
    for q in range(TERMS):
        weights = jnp.where((row == 1) & (lane == q), params_ref[0, q], weights)
    high = weights.astype(bf16).astype(f32)
    rest = weights - high
    mid = rest.astype(bf16).astype(f32)
    low = (rest - mid).astype(bf16).astype(f32)
    b = jnp.where(row == 0, b + pltpu.roll(b, 6, 0), 0.0)
    b = in_two(b).astype(f32) + (high + pltpu.roll(mid, TERMS, 1) + pltpu.roll(low, 2 * TERMS, 1))
    a = a.astype(bf16)
    b = b.astype(bf16)

    def spread(m, _):
        out_ref[m, 0:16, :] = a
        out_ref[m, 16:24, :] = b
        return 0

    lax.fori_loop(0, CHIPS, spread, 0, unroll=8)


def total(params, parts):
    vm = pl.BlockSpec(memory_space=pltpu.VMEM)
    return pl.pallas_call(
        total_body,
        in_specs=[pl.BlockSpec(memory_space=pltpu.SMEM), vm],
        out_shape=jax.ShapeDtypeStruct((CHIPS, CHUNK, NZ), bf16),
        name="total",
    )(params, parts)


def solve_body(core_ref, own_ref, other_ref, order_ref, out_ref, st, high, low, extra, weight, wide, scale, xs, rs, ps):
    c = core_ref[0]
    half = TERMS * K // 2

    def place(g, _):
        mine = pl.multiple_of(c * half + g * 16, 16)
        theirs = pl.multiple_of((1 - c) * half + g * 16, 16)
        for l in range(M // NZ):
            st[pl.ds(mine, 16), l * NZ:(l + 1) * NZ] = own_ref[g * 8 + l, 0:16, :]
            st[pl.ds(theirs, 16), l * NZ:(l + 1) * NZ] = other_ref[g * 8 + l, 0:16, :]
        return 0

    lax.fori_loop(0, half // 16, place, 0)

    for ref, h in ((own_ref, c), (other_ref, 1 - c)):
        def lift(m, _):
            extra[pl.ds(pl.multiple_of(m * 8, 8), 8), :] = ref[m, 16:24, :].astype(f32)
            return 0

        lax.fori_loop(0, CHIPS, lift, 0, unroll=8)
        e = extra[pl.ds(1, CHIPS, stride=8), :]
        e = e + (pltpu.roll(e, NZ - TERMS, 1) + pltpu.roll(e, NZ - 2 * TERMS, 1))
        for q in range(TERMS):
            weight[q, pl.ds(pl.multiple_of(h * CHIPS, CHIPS), CHIPS), :] = jnp.broadcast_to(e[:, q:q + 1], (CHIPS, K))
    source = jnp.concatenate([own_ref[l, 16:24, :] for l in range(M // NZ)], axis=1)
    row = lax.broadcasted_iota(jnp.int32, (8, M), 0)
    source = jnp.where((row == 0) | (row == 2), source.astype(f32), 0.0).astype(bf16)
    gram = nt(st[...], st[...])
    projected = nt(source, st[...])
    projected = projected[0:1, :] + projected[2:3, :]
    top = gram.astype(bf16)
    high[...] = top
    low[...] = (gram - top.astype(f32)).astype(bf16)
    diagonal = lax.broadcasted_iota(jnp.int32, (K, K), 0) == lax.broadcasted_iota(jnp.int32, (K, K), 1)
    sizes = jnp.zeros((POINTS, K), f32)
    right = jnp.zeros((POINTS, K), f32)
    for q in range(TERMS):
        right = right + weight[q] * projected[:, q * K:(q + 1) * K]
        for r in range(TERMS):
            block = gram[q * K:(q + 1) * K, r * K:(r + 1) * K]
            entries = jnp.sum(jnp.where(diagonal, block, 0.0), axis=0, keepdims=True)
            sizes = sizes + (weight[q] * weight[r]) * entries
    scale[...] = 1.0 / sizes
    z0 = right * scale[...]
    xs[...] = jnp.zeros((POINTS, K), f32)
    rs[...] = right
    ps[...] = z0
    start = jnp.sum(right * z0, axis=1, keepdims=True)
    goal = start * TOL2

    def step(rz):
        p = ps[...]
        for q in range(TERMS):
            t = weight[q] * p
            t_high = t.astype(bf16)
            wide[0:POINTS, q * K:(q + 1) * K] = t_high
            wide[POINTS:2 * POINTS, q * K:(q + 1) * K] = (t - t_high.astype(f32)).astype(bf16)
        both = jnp.dot(wide[...], high[...], preferred_element_type=f32)
        image = both[:POINTS] + both[POINTS:] + jnp.dot(wide[0:POINTS, :], low[...], preferred_element_type=f32)
        ap = weight[0] * image[:, 0:K]
        for q in range(1, TERMS):
            ap = ap + weight[q] * image[:, q * K:(q + 1) * K]
        pap = jnp.sum(p * ap, axis=1, keepdims=True)
        alpha = jnp.where(pap > 0.0, rz / pap, 0.0)
        xs[...] += alpha * p
        r = rs[...] - alpha * ap
        rs[...] = r
        z = r * scale[...]
        new = jnp.sum(r * z, axis=1, keepdims=True)
        beta = jnp.where(rz > 0.0, new / rz, 0.0)
        ps[...] = z + beta * p
        return new

    def rounds(carry):
        n, rz, _ = carry
        rz = step(step(rz))
        return (n + 1, rz, jnp.max(jnp.where(rz > goal, 1.0, 0.0)))

    lax.while_loop(lambda s: (s[0] < MAX_ROUNDS) & (s[2] > 0.5), rounds, (jnp.int32(0), start, f32(1.0)))
    wanted = order_ref[...]
    wanted = (wanted & 1) * CHIPS + (wanted >> 1)
    pick = jnp.where(lax.broadcasted_iota(jnp.int32, (POINTS, POINTS), 0) == wanted, 1.0, 0.0).astype(bf16)
    coef = xs[...].astype(bf16)
    picked = lax.dot_general(pick, coef, (((0,), (0,)), ((), ())), preferred_element_type=f32)
    out_ref[...] = picked.astype(bf16)


def solve(core, own, other, order):
    vm = pl.BlockSpec(memory_space=pltpu.VMEM)
    wide = (POINTS, K)
    return pl.pallas_call(
        solve_body,
        in_specs=[pl.BlockSpec(memory_space=pltpu.SMEM), vm, vm, vm],
        out_shape=jax.ShapeDtypeStruct((POINTS, K), bf16),
        scratch_shapes=[
            pltpu.VMEM((TERMS * K, M), bf16),
            pltpu.VMEM((TERMS * K, TERMS * K), bf16),
            pltpu.VMEM((TERMS * K, TERMS * K), bf16),
            pltpu.VMEM((CHIPS * 8, NZ), f32),
            pltpu.VMEM((TERMS, POINTS, K), f32),
            pltpu.VMEM((2 * POINTS, TERMS * K), bf16),
            pltpu.VMEM(wide, f32),
            pltpu.VMEM(wide, f32),
            pltpu.VMEM(wide, f32),
            pltpu.VMEM(wide, f32),
        ],
        compiler_params=pltpu.CompilerParams(vmem_limit_bytes=56 << 20),
        name="solve",
    )(core, own, other, order)


def fields_body(picked_ref, bt_ref, out_ref, turned):
    got = jnp.dot(picked_ref[...], bt_ref[0], preferred_element_type=f32)
    for y in range(NY):
        turned[pl.ds(y, POINTS, stride=NY), :] = got[:, y * NZ:(y + 1) * NZ]
    out_ref[...] = turned[...].reshape(POINTS, 1, NY, NZ).astype(bf16)


def fields_of(picked, bt):
    return pl.pallas_call(
        fields_body,
        grid=(NX,),
        in_specs=[
            pl.BlockSpec((POINTS, K), lambda x: (0, 0)),
            pl.BlockSpec((1, K, CELLS), lambda x: (x, 0, 0)),
        ],
        out_specs=pl.BlockSpec((POINTS, 1, NY, NZ), lambda x: (0, x, 0, 0)),
        out_shape=jax.ShapeDtypeStruct((POINTS, NX, NY, NZ), bf16),
        scratch_shapes=[pltpu.VMEM((POINTS * NY, NZ), f32)],
        compiler_params=pltpu.CompilerParams(
            dimension_semantics=("arbitrary",), vmem_limit_bytes=48 << 20
        ),
        name="fields",
    )(picked, bt)


NARROW = ("x", "zl")
WIDE = ("y", "zh", "core")
CHIP = ("x", "zl", "y", "zh")


def halo_infos(rows, signs, coeffs):
    out = []
    for axes, count, dim, term in ((NARROW, 8, 1, 1), (WIDE, 32, 2, 2)):
        last = rows.shape[dim] - 1

        def info(at):
            take = lambda a: lax.index_in_dim(a, at, dim, keepdims=False).astype(f32)
            return jnp.concatenate([take(rows), take(signs), take(coeffs)[term:term + 1]], axis=0)

        up = [(i, i + 1) for i in range(count - 1)]
        down = [(i + 1, i) for i in range(count - 1)]
        out.append(lax.ppermute(info(last), axes, up))
        out.append(lax.ppermute(info(0), axes, down))
    return out


def per_device(basis, rhs, coeffs, rows, signs, params, order):
    infos = halo_infos(rows, signs, coeffs)
    core = lax.axis_index("core").astype(jnp.int32).reshape(1)
    acc, bt = sketch(basis, rhs, coeffs, rows, signs)
    own, other = edges(core, acc, bt, infos)
    swap = [(0, 1), (1, 0)]
    got = lax.ppermute(other, "core", swap)
    parts = lax.all_to_all(merge(own, got), CHIP, 0, 0, tiled=True)
    mine = lax.all_to_all(total(params, parts), CHIP, 0, 0, tiled=True)
    theirs = lax.ppermute(mine, "core", swap)
    picked = solve(core, mine, theirs, order.reshape(1, POINTS))
    return fields_of(picked, bt)


def solution(mesh):
    fine = Mesh(mesh.devices.reshape(4, 2, 4, 4, 2), ("x", "zl", "y", "zh", "core"))
    cells = P(None, NARROW, WIDE, None)
    in_specs = (
        cells,
        P(NARROW, WIDE, None),
        cells,
        cells,
        cells,
        P(NARROW + WIDE, None),
        P(),
    )
    return jax.shard_map(per_device, mesh=fine, in_specs=in_specs, out_specs=cells, check_vma=False)
```

```python
import jax
import jax.numpy as jnp
from jax import lax
from jax.experimental import pallas as pl
from jax.experimental.pallas import tpu as pltpu
from jax.sharding import Mesh
from jax.sharding import PartitionSpec as P

K = 128
M = 1024
TERMS = 4
NNZ = 4
ROWS = M // NNZ
NX = 4
NY = 16
NZ = 128
CELLS = NY * NZ
TALL = TERMS * K + 16
CHIPS = 128
SIDE = 16
DEEP = 8
BODY = 128
CHUNK = BODY + 8
POINTS = 256
TOL2 = 1e-10
MAX_ROUNDS = 256

f32 = jnp.float32
bf16 = jnp.bfloat16


def put_hash(hash_ref, slot_ref, y, row_of, sign_of):
    for j in range(NNZ):
        row = jnp.broadcast_to(row_of(j), (16, NZ)).astype(bf16)
        sign = jnp.broadcast_to(sign_of(j), (16, NZ)).astype(bf16)
        for s in range(0, ROWS, 16):
            hash_ref[y, j * ROWS + s:j * ROWS + s + 16, :] = jnp.where(
                slot_ref[s:s + 16, :] == row, sign, jnp.zeros((16, NZ), bf16)
            )


def put_slots(slot_ref):
    slot_ref[...] = lax.broadcasted_iota(jnp.int32, (ROWS, NZ), 0).astype(f32).astype(bf16)


def nt(a, b):
    return lax.dot_general(a, b, (((1,), (1,)), ((), ())), preferred_element_type=f32)


def side_by_side(ref, count):
    return jnp.concatenate([ref[y] for y in range(count)], axis=1)


def in_three(extra):
    high = extra.astype(bf16).astype(f32)
    rest = extra - high
    mid = rest.astype(bf16).astype(f32)
    return (high + pltpu.roll(mid, 2, 0) + pltpu.roll(rest - mid, 4, 0)).astype(bf16)


def from_three(coded):
    coded = coded.astype(f32)
    row = lax.broadcasted_iota(jnp.int32, (8, NZ), 0)
    return jnp.where(row < 2, coded + (pltpu.roll(coded, 6, 0) + pltpu.roll(coded, 4, 0)), 0.0)


def sketch_body(basis_ref, rhs_ref, co_ref, rows_ref, signs_ref, acc_ref, bt_ref, pad, terms, hashes, source_ref, slots):
    put_slots(slots)
    none = jnp.zeros((NY + 2, K, NZ), f32)
    pad[0] = none
    pad[NX + 1] = none
    for x in range(NX):
        pad[x + 1, 0] = jnp.zeros((K, NZ), f32)
        pad[x + 1, NY + 1] = jnp.zeros((K, NZ), f32)
    out = lax.broadcasted_iota(jnp.int32, (16 * NY, 16 * NY), 0)
    src = lax.broadcasted_iota(jnp.int32, (16 * NY, 16 * NY), 1)
    turn = jnp.where((out // 16 == src % 16) & (out % 16 == src // 16), 1.0, 0.0).astype(bf16)

    def turned(i, _):
        k = pl.multiple_of(i * 16, 16)
        for x in range(0, NX, 2):
            both = jnp.concatenate(
                [basis_ref[pl.ds(k, 16), x + d].reshape(16 * NY, NZ) for d in range(2)], axis=1
            )
            got = jnp.dot(turn, both, preferred_element_type=f32)
            for d in range(2):
                for y in range(NY):
                    tile = got[y * 16:(y + 1) * 16, d * NZ:(d + 1) * NZ]
                    pad[x + d + 1, y + 1, pl.ds(k, 16), :] = tile
                    bt_ref[x + d, y, pl.ds(k, 16), :] = tile.astype(bf16)
        return 0

    lax.fori_loop(0, K // 16, turned, 0)
    lane = lax.broadcasted_iota(jnp.int32, (1, NZ), 1)

    def plane(x, _):
        source_ref[...] = rhs_ref[x].astype(f32)

        def group(y, _):
            c0, c1, c2, c3 = (co_ref[q, x, pl.ds(y, 1), :] for q in range(TERMS))
            low3 = jnp.where(lane == 0, 0.0, c3)
            up3 = jnp.where(lane == NZ - 1, 0.0, c3)
            for k in range(0, K, 16):
                at = slice(k, k + 16)
                v = pad[x + 1, y + 1, at, :]
                v2 = v + v
                along_x = v2 - pad[x, y + 1, at, :] - pad[x + 2, y + 1, at, :]
                along_y = v2 - pad[x + 1, y, at, :] - pad[x + 1, y + 2, at, :]
                t3 = c3 * v2 - low3 * pltpu.roll(v, 1, 1) - up3 * pltpu.roll(v, NZ - 1, 1)
                for q, t in enumerate((c0 * v, c1 * along_x, c2 * along_y, t3)):
                    terms[y, q * K + k:q * K + k + 16, :] = t.astype(bf16)
            top = lax.broadcasted_iota(jnp.int32, (16, NZ), 0) == 0
            source = source_ref[pl.ds(y, 1), :]
            terms[y, TERMS * K:TALL, :] = jnp.where(top, source, 0.0).astype(bf16)
            put_hash(
                hashes,
                slots,
                y,
                lambda j: rows_ref[j, x, pl.ds(y, 1), :].astype(f32),
                lambda j: signs_ref[j, x, pl.ds(y, 1), :].astype(f32) - 0.5,
            )
            return 0

        lax.fori_loop(0, NY, group, 0, unroll=2)
        got = nt(side_by_side(terms, NY), side_by_side(hashes, NY))

        @pl.when(x == 0)
        def _():
            acc_ref[...] = got

        @pl.when(x > 0)
        def _():
            acc_ref[...] += got

        return 0

    lax.fori_loop(0, NX, plane, 0)


def sketch(basis, rhs, coeffs, rows, signs):
    return pl.pallas_call(
        sketch_body,
        out_shape=(
            jax.ShapeDtypeStruct((TALL, M), f32),
            jax.ShapeDtypeStruct((NX, NY, K, NZ), bf16),
        ),
        scratch_shapes=[
            pltpu.VMEM((NX + 2, NY + 2, K, NZ), f32),
            pltpu.VMEM((NY, TALL, NZ), bf16),
            pltpu.VMEM((NY, M, NZ), bf16),
            pltpu.VMEM((NY, NZ), f32),
            pltpu.VMEM((ROWS, NZ), bf16),
        ],
        compiler_params=pltpu.CompilerParams(vmem_limit_bytes=56 << 20),
        name="sketch",
    )(basis, rhs, coeffs, rows, signs)


def planes_body(rows_ref, signs_ref, co_ref, x_low, x_high, y_low, y_high):
    for out, x in ((x_low, 0), (x_high, NX - 1)):
        out[0:NNZ] = rows_ref[:, x].astype(f32)
        out[NNZ:2 * NNZ] = signs_ref[:, x].astype(f32)
        out[2 * NNZ] = co_ref[1, x]
    for out, y in ((y_low, 0), (y_high, NY - 1)):
        for x in range(NX):
            for j in range(NNZ):
                out[j, x:x + 1, :] = rows_ref[j, x, y:y + 1, :].astype(f32)
                out[NNZ + j, x:x + 1, :] = signs_ref[j, x, y:y + 1, :].astype(f32)
            out[2 * NNZ, x:x + 1, :] = co_ref[2, x, y:y + 1, :]


def planes(rows, signs, coeffs):
    along_x = jax.ShapeDtypeStruct((2 * NNZ + 1, NY, NZ), f32)
    along_y = jax.ShapeDtypeStruct((2 * NNZ + 1, NX, NZ), f32)
    return pl.pallas_call(
        planes_body, out_shape=(along_x, along_x, along_y, along_y), name="planes"
    )(rows, signs, coeffs)


def edge_body(ids_ref, acc_in, bxl_ref, bxu_ref, byl_ref, byu_ref, xl_ref, xu_ref, yl_ref, yu_ref, own_ref, other_ref, acc, terms, hashes, slots):
    put_slots(slots)
    acc[...] = acc_in[...]

    def one(info, v, y_info, place):
        terms[place] = (-info[2 * NNZ, pl.ds(y_info, 1), :] * v.astype(f32)).astype(bf16)
        put_hash(
            hashes,
            slots,
            place,
            lambda j: info[j, pl.ds(y_info, 1), :],
            lambda j: info[NNZ + j, pl.ds(y_info, 1), :] - 0.5,
        )

    for info, values in ((xl_ref, bxl_ref), (xu_ref, bxu_ref)):
        def group(y, _):
            one(info, values[0, y], y, y)
            return 0

        lax.fori_loop(0, NY, group, 0, unroll=2)
        acc[K:2 * K, :] += nt(side_by_side(terms, NY), side_by_side(hashes, NY))

    def group(x, _):
        one(yl_ref, byl_ref[x, 0], x, x)
        one(yu_ref, byu_ref[x, 0], x, NX + x)
        return 0

    lax.fori_loop(0, NX, group, 0)
    acc[2 * K:3 * K, :] += nt(side_by_side(terms, 2 * NX), side_by_side(hashes, 2 * NX))
    c = ids_ref[0]
    row = lax.broadcasted_iota(jnp.int32, (8, NZ), 0)

    def split(i, _):
        mine = pl.multiple_of(c * 2 * K + i * 16, 16)
        theirs = pl.multiple_of((1 - c) * 2 * K + i * 16, 16)
        for l in range(M // NZ):
            own_ref[i, l * 16:l * 16 + 16, :] = acc[pl.ds(mine, 16), l * NZ:(l + 1) * NZ]
            other_ref[i, l * 16:l * 16 + 16, :] = acc[pl.ds(theirs, 16), l * NZ:(l + 1) * NZ].astype(bf16)
        lane = pl.multiple_of(jnp.minimum(i, M // NZ - 1) * NZ, NZ)
        source = acc[TERMS * K:TERMS * K + 8, pl.ds(lane, NZ)]
        source = jnp.where((row == 0) & (i < M // NZ), source, 0.0)
        own_ref[i, BODY:CHUNK, :] = source
        other_ref[i, BODY:CHUNK, :] = in_three(source)
        return 0

    lax.fori_loop(0, SIDE, split, 0)


def edges(ids, acc, bt, infos):
    vm = pl.BlockSpec(memory_space=pltpu.VMEM)
    return pl.pallas_call(
        edge_body,
        grid=(1,),
        in_specs=[
            pl.BlockSpec(memory_space=pltpu.SMEM),
            vm,
            pl.BlockSpec((1, NY, K, NZ), lambda i: (0, 0, 0, 0)),
            pl.BlockSpec((1, NY, K, NZ), lambda i: (NX - 1, 0, 0, 0)),
            pl.BlockSpec((NX, 1, K, NZ), lambda i: (0, 0, 0, 0)),
            pl.BlockSpec((NX, 1, K, NZ), lambda i: (0, NY - 1, 0, 0)),
            vm,
            vm,
            vm,
            vm,
        ],
        out_specs=(vm, vm),
        out_shape=(
            jax.ShapeDtypeStruct((SIDE, CHUNK, NZ), f32),
            jax.ShapeDtypeStruct((SIDE, CHUNK, NZ), bf16),
        ),
        scratch_shapes=[
            pltpu.VMEM((TALL, M), f32),
            pltpu.VMEM((NY, K, NZ), bf16),
            pltpu.VMEM((NY, M, NZ), bf16),
            pltpu.VMEM((ROWS, NZ), bf16),
        ],
        compiler_params=pltpu.CompilerParams(vmem_limit_bytes=56 << 20),
        name="edges",
    )(ids, acc, bt, bt, bt, bt, *infos)


def merge_body(own_ref, got_ref, out_ref):
    def add(i, _):
        out_ref[i, 0:BODY, :] = (own_ref[i, 0:BODY, :] + got_ref[i, 0:BODY, :].astype(f32)).astype(bf16)
        out_ref[i, BODY:CHUNK, :] = in_three(own_ref[i, BODY:CHUNK, :] + from_three(got_ref[i, BODY:CHUNK, :]))
        return 0

    lax.fori_loop(0, SIDE, add, 0)


def merge(own, got):
    return pl.pallas_call(
        merge_body,
        out_shape=jax.ShapeDtypeStruct((SIDE, CHUNK, NZ), bf16),
        name="merge",
    )(own, got)


def total_of(parts_ref, out_ref, count, copies):
    for at in range(0, BODY, 64):
        total = parts_ref[0, at:at + 64, :].astype(f32)
        for i in range(1, count):
            total = total + parts_ref[i, at:at + 64, :].astype(f32)
        total = total.astype(bf16)
        for i in range(copies):
            out_ref[i, at:at + 64, :] = total
    extra = from_three(parts_ref[0, BODY:CHUNK, :])
    for i in range(1, count):
        extra = extra + from_three(parts_ref[i, BODY:CHUNK, :])
    return extra


def first_body(ids_ref, params_ref, parts_ref, out_ref):
    extra = total_of(parts_ref, out_ref, SIDE, DEEP)
    lane = lax.broadcasted_iota(jnp.int32, (8, NZ), 1)
    row = lax.broadcasted_iota(jnp.int32, (8, NZ), 0)
    extra = jnp.where(row == 0, extra, 0.0)
    for q in range(TERMS):
        extra = jnp.where((row == 1) & (lane == q * DEEP + ids_ref[1]), params_ref[0, q], extra)
    extra = in_three(extra)
    for i in range(DEEP):
        out_ref[i, BODY:CHUNK, :] = extra


def first(ids, params, parts):
    sm = pl.BlockSpec(memory_space=pltpu.SMEM)
    return pl.pallas_call(
        first_body,
        in_specs=[sm, sm, pl.BlockSpec(memory_space=pltpu.VMEM)],
        out_shape=jax.ShapeDtypeStruct((DEEP, CHUNK, NZ), bf16),
        name="first",
    )(ids, params, parts)


def second_body(parts_ref, out_ref):
    extra = in_three(total_of(parts_ref, out_ref, DEEP, SIDE))
    for i in range(SIDE):
        out_ref[i, BODY:CHUNK, :] = extra


def second(parts):
    return pl.pallas_call(
        second_body,
        out_shape=jax.ShapeDtypeStruct((SIDE, CHUNK, NZ), bf16),
        name="second",
    )(parts)


def solve_body(ids_ref, own_ref, other_ref, order_ref, out_ref, st, high, low, extra, weight, wide, scale, xs, rs, ps):
    c = ids_ref[0]
    half = TERMS * K // 2

    def place(i, _):
        mine = pl.multiple_of(c * half + i * 16, 16)
        theirs = pl.multiple_of((1 - c) * half + i * 16, 16)
        for l in range(M // NZ):
            st[pl.ds(mine, 16), l * NZ:(l + 1) * NZ] = own_ref[i, l * 16:l * 16 + 16, :]
            st[pl.ds(theirs, 16), l * NZ:(l + 1) * NZ] = other_ref[i, l * 16:l * 16 + 16, :]
        return 0

    lax.fori_loop(0, SIDE, place, 0)
    extra[...] = jnp.zeros((NZ, NZ), f32)
    for ref, h in ((own_ref, c), (other_ref, 1 - c)):
        for i in range(SIDE):
            extra[i:i + 1, :] = from_three(ref[i, BODY:CHUNK, :])[1:2, :]
        columns = jnp.transpose(extra[...])
        for i in range(SIDE):
            at = pl.multiple_of(h * CHIPS + i * DEEP, DEEP)
            for q in range(TERMS):
                weight[q, pl.ds(at, DEEP), :] = jnp.broadcast_to(
                    columns[q * DEEP:(q + 1) * DEEP, i:i + 1], (DEEP, K)
                )
    source = jnp.concatenate([own_ref[i, BODY:CHUNK, :] for i in range(M // NZ)], axis=1)
    gram = nt(st[...], st[...])
    projected = nt(source, st[...])
    projected = projected[0:1, :] + (projected[2:3, :] + projected[4:5, :])
    top = gram.astype(bf16)
    high[...] = top
    low[...] = (gram - top.astype(f32)).astype(bf16)
    diagonal = lax.broadcasted_iota(jnp.int32, (K, K), 0) == lax.broadcasted_iota(jnp.int32, (K, K), 1)
    sizes = jnp.zeros((POINTS, K), f32)
    right = jnp.zeros((POINTS, K), f32)
    for q in range(TERMS):
        right = right + weight[q] * projected[:, q * K:(q + 1) * K]
        for r in range(TERMS):
            block = gram[q * K:(q + 1) * K, r * K:(r + 1) * K]
            entries = jnp.sum(jnp.where(diagonal, block, 0.0), axis=0, keepdims=True)
            sizes = sizes + (weight[q] * weight[r]) * entries
    scale[...] = 1.0 / sizes
    z0 = right * scale[...]
    xs[...] = jnp.zeros((POINTS, K), f32)
    rs[...] = right
    ps[...] = z0
    start = jnp.sum(right * z0, axis=1, keepdims=True)
    goal = start * TOL2

    def step(rz):
        p = ps[...]
        for q in range(TERMS):
            t = weight[q] * p
            t_high = t.astype(bf16)
            wide[0:POINTS, q * K:(q + 1) * K] = t_high
            wide[POINTS:2 * POINTS, q * K:(q + 1) * K] = (t - t_high.astype(f32)).astype(bf16)
        both = jnp.dot(wide[...], high[...], preferred_element_type=f32)
        image = both[:POINTS] + both[POINTS:] + jnp.dot(wide[0:POINTS, :], low[...], preferred_element_type=f32)
        ap = weight[0] * image[:, 0:K]
        for q in range(1, TERMS):
            ap = ap + weight[q] * image[:, q * K:(q + 1) * K]
        pap = jnp.sum(p * ap, axis=1, keepdims=True)
        alpha = jnp.where(pap > 0.0, rz / pap, 0.0)
        xs[...] += alpha * p
        r = rs[...] - alpha * ap
        rs[...] = r
        z = r * scale[...]
        new = jnp.sum(r * z, axis=1, keepdims=True)
        beta = jnp.where(rz > 0.0, new / rz, 0.0)
        ps[...] = z + beta * p
        return new

    def rounds(carry):
        n, rz, _ = carry
        rz = step(step(rz))
        return (n + 1, rz, jnp.max(jnp.where(rz > goal, 1.0, 0.0)))

    lax.while_loop(lambda s: (s[0] < MAX_ROUNDS) & (s[2] > 0.5), rounds, (jnp.int32(0), start, f32(1.0)))
    wanted = order_ref[...]
    wanted = (
        ((wanted & 1) << 7)
        + ((wanted >> 6) << 5)
        + (((wanted >> 3) & 3) << 3)
        + (((wanted >> 5) & 1) << 2)
        + ((wanted >> 1) & 3)
    )
    pick = jnp.where(lax.broadcasted_iota(jnp.int32, (POINTS, POINTS), 0) == wanted, 1.0, 0.0).astype(bf16)
    coef = xs[...].astype(bf16)
    picked = lax.dot_general(pick, coef, (((0,), (0,)), ((), ())), preferred_element_type=f32)
    out_ref[...] = picked.astype(bf16)


def solve(ids, own, other, order):
    vm = pl.BlockSpec(memory_space=pltpu.VMEM)
    wide = (POINTS, K)
    return pl.pallas_call(
        solve_body,
        in_specs=[pl.BlockSpec(memory_space=pltpu.SMEM), vm, vm, vm],
        out_shape=jax.ShapeDtypeStruct((POINTS, K), bf16),
        scratch_shapes=[
            pltpu.VMEM((TERMS * K, M), bf16),
            pltpu.VMEM((TERMS * K, TERMS * K), bf16),
            pltpu.VMEM((TERMS * K, TERMS * K), bf16),
            pltpu.VMEM((NZ, NZ), f32),
            pltpu.VMEM((TERMS, POINTS, K), f32),
            pltpu.VMEM((2 * POINTS, TERMS * K), bf16),
            pltpu.VMEM(wide, f32),
            pltpu.VMEM(wide, f32),
            pltpu.VMEM(wide, f32),
            pltpu.VMEM(wide, f32),
        ],
        compiler_params=pltpu.CompilerParams(vmem_limit_bytes=56 << 20),
        name="solve",
    )(ids, own, other, order)


def fields_body(picked_ref, bt_ref, out_ref, turned):
    picked = picked_ref[...]
    for y in range(0, NY, 2):
        pair = jnp.concatenate([bt_ref[0, y], bt_ref[0, y + 1]], axis=1)
        got = jnp.dot(picked, pair, preferred_element_type=f32)
        for d in range(2):
            turned[pl.ds(y + d, POINTS, stride=NY), :] = got[:, d * NZ:(d + 1) * NZ]
    out_ref[...] = turned[...].reshape(POINTS, 1, NY, NZ).astype(bf16)


def fields_of(picked, bt):
    return pl.pallas_call(
        fields_body,
        grid=(NX,),
        in_specs=[
            pl.BlockSpec((POINTS, K), lambda x: (0, 0)),
            pl.BlockSpec((1, NY, K, NZ), lambda x: (x, 0, 0, 0)),
        ],
        out_specs=pl.BlockSpec((POINTS, 1, NY, NZ), lambda x: (0, x, 0, 0)),
        out_shape=jax.ShapeDtypeStruct((POINTS, NX, NY, NZ), bf16),
        scratch_shapes=[pltpu.VMEM((POINTS * NY, NZ), f32)],
        compiler_params=pltpu.CompilerParams(
            dimension_semantics=("arbitrary",), vmem_limit_bytes=48 << 20
        ),
        name="fields",
    )(picked, bt)


NARROW = ("x", "zl")
WIDE = ("y", "zh", "core")
FACE = ("x", "y")
DEPTH = ("zl", "zh")


def per_device(basis, rhs, coeffs, rows, signs, params, order):
    x_low, x_high, y_low, y_high = planes(rows, signs, coeffs)
    infos = []
    for axes, count, low, high in ((NARROW, 8, x_low, x_high), (WIDE, 32, y_low, y_high)):
        infos.append(lax.ppermute(high, axes, [(i, i + 1) for i in range(count - 1)]))
        infos.append(lax.ppermute(low, axes, [(i + 1, i) for i in range(count - 1)]))
    core = lax.axis_index("core").astype(jnp.int32)
    ids = jnp.stack([core, (lax.axis_index("zl") * 4 + lax.axis_index("zh")).astype(jnp.int32)])
    acc, bt = sketch(basis, rhs, coeffs, rows, signs)
    own, other = edges(ids, acc, bt, infos)
    swap = [(0, 1), (1, 0)]
    parts = merge(own, lax.ppermute(other, "core", swap))
    parts = lax.all_to_all(parts, FACE, 0, 0, tiled=True)
    parts = lax.all_to_all(first(ids, params, parts), DEPTH, 0, 0, tiled=True)
    mine = lax.all_to_all(second(parts), FACE, 0, 0, tiled=True)
    theirs = lax.ppermute(mine, "core", swap)
    picked = solve(ids, mine, theirs, order.reshape(1, POINTS))
    return fields_of(picked, bt)


def solution(mesh):
    fine = Mesh(mesh.devices.reshape(4, 2, 4, 4, 2), ("x", "zl", "y", "zh", "core"))
    cells = P(None, NARROW, WIDE, None)
    in_specs = (
        cells,
        P(NARROW, WIDE, None),
        cells,
        cells,
        cells,
        P(NARROW + WIDE, None),
        P(),
    )
    return jax.shard_map(per_device, mesh=fine, in_specs=in_specs, out_specs=cells, check_vma=False)
```

```python
import jax
import jax.numpy as jnp
from jax import lax
from jax.experimental import pallas as pl
from jax.experimental.pallas import tpu as pltpu
from jax.sharding import Mesh
from jax.sharding import PartitionSpec as P

K = 128
M = 1024
TERMS = 4
NNZ = 4
ROWS = M // NNZ
NX = 4
NY = 16
NZ = 128
CELLS = NY * NZ
TALL = TERMS * K + 16
CHIPS = 128
SIDE = 16
DEEP = 8
BODY = 128
CHUNK = BODY + 8
POINTS = 256
TOL2 = 1e-10
MAX_ROUNDS = 256
PAIRS = tuple((q, r) for q in range(TERMS) for r in range(q, TERMS))

f32 = jnp.float32
bf16 = jnp.bfloat16


def put_hash(hash_ref, slot_ref, y, row_of, sign_of):
    for j in range(NNZ):
        row = jnp.broadcast_to(row_of(j), (16, NZ)).astype(bf16)
        sign = jnp.broadcast_to(sign_of(j), (16, NZ)).astype(bf16)
        for s in range(0, ROWS, 16):
            hash_ref[y, j * ROWS + s:j * ROWS + s + 16, :] = jnp.where(
                slot_ref[s:s + 16, :] == row, sign, jnp.zeros((16, NZ), bf16)
            )


def put_slots(slot_ref):
    slot_ref[...] = lax.broadcasted_iota(jnp.int32, (ROWS, NZ), 0).astype(f32).astype(bf16)


def nt(a, b):
    return lax.dot_general(a, b, (((1,), (1,)), ((), ())), preferred_element_type=f32)


def side_by_side(ref, count):
    return jnp.concatenate([ref[y] for y in range(count)], axis=1)


def in_three(extra):
    high = extra.astype(bf16).astype(f32)
    rest = extra - high
    mid = rest.astype(bf16).astype(f32)
    return (high + pltpu.roll(mid, 2, 0) + pltpu.roll(rest - mid, 4, 0)).astype(bf16)


def from_three(coded):
    coded = coded.astype(f32)
    row = lax.broadcasted_iota(jnp.int32, (8, NZ), 0)
    return jnp.where(row < 2, coded + (pltpu.roll(coded, 6, 0) + pltpu.roll(coded, 4, 0)), 0.0)


def sketch_body(
    basis_ref, rhs_ref, co_hbm, rows_hbm, signs_hbm, acc_ref, bt_hbm,
    pad, terms, hashes, source_ref, slots, co_ref, rows_ref, signs_ref, bt_ref, sems,
):
    fetches = [
        pltpu.make_async_copy(src, dst, sems.at[i])
        for i, (src, dst) in enumerate(((co_hbm, co_ref), (rows_hbm, rows_ref), (signs_hbm, signs_ref)))
    ]
    for fetch in fetches:
        fetch.start()
    put_slots(slots)
    none = jnp.zeros((NY + 2, K, NZ), f32)
    pad[0] = none
    pad[NX + 1] = none
    for x in range(NX):
        pad[x + 1, 0] = jnp.zeros((K, NZ), f32)
        pad[x + 1, NY + 1] = jnp.zeros((K, NZ), f32)
    out = lax.broadcasted_iota(jnp.int32, (16 * NY, 16 * NY), 0)
    src = lax.broadcasted_iota(jnp.int32, (16 * NY, 16 * NY), 1)
    turn = jnp.where((out // 16 == src % 16) & (out % 16 == src // 16), 1.0, 0.0).astype(bf16)

    def turned(i, _):
        k = pl.multiple_of(i * 16, 16)
        for x in range(0, NX, 2):
            both = jnp.concatenate(
                [basis_ref[pl.ds(k, 16), x + d].reshape(16 * NY, NZ) for d in range(2)], axis=1
            )
            got = jnp.dot(turn, both, preferred_element_type=f32)
            for d in range(2):
                for y in range(NY):
                    tile = got[y * 16:(y + 1) * 16, d * NZ:(d + 1) * NZ]
                    pad[x + d + 1, y + 1, pl.ds(k, 16), :] = tile
                    bt_ref[x + d, y, pl.ds(k, 16), :] = tile.astype(bf16)
        return 0

    lax.fori_loop(0, K // 16, turned, 0)
    give = pltpu.make_async_copy(bt_ref, bt_hbm, sems.at[3])
    give.start()
    for fetch in fetches:
        fetch.wait()
    lane = lax.broadcasted_iota(jnp.int32, (1, NZ), 1)

    def plane(x, _):
        source_ref[...] = rhs_ref[x].astype(f32)

        def group(y, _):
            c0, c1, c2, c3 = (co_ref[q, x, pl.ds(y, 1), :] for q in range(TERMS))
            low3 = jnp.where(lane == 0, 0.0, c3)
            up3 = jnp.where(lane == NZ - 1, 0.0, c3)
            for k in range(0, K, 16):
                at = slice(k, k + 16)
                v = pad[x + 1, y + 1, at, :]
                v2 = v + v
                along_x = v2 - pad[x, y + 1, at, :] - pad[x + 2, y + 1, at, :]
                along_y = v2 - pad[x + 1, y, at, :] - pad[x + 1, y + 2, at, :]
                t3 = c3 * v2 - low3 * pltpu.roll(v, 1, 1) - up3 * pltpu.roll(v, NZ - 1, 1)
                for q, t in enumerate((c0 * v, c1 * along_x, c2 * along_y, t3)):
                    terms[y, q * K + k:q * K + k + 16, :] = t.astype(bf16)
            top = lax.broadcasted_iota(jnp.int32, (16, NZ), 0) == 0
            source = source_ref[pl.ds(y, 1), :]
            terms[y, TERMS * K:TALL, :] = jnp.where(top, source, 0.0).astype(bf16)
            put_hash(
                hashes,
                slots,
                y,
                lambda j: rows_ref[j, x, pl.ds(y, 1), :].astype(f32),
                lambda j: signs_ref[j, x, pl.ds(y, 1), :].astype(f32) - 0.5,
            )
            return 0

        lax.fori_loop(0, NY, group, 0, unroll=2)
        got = nt(side_by_side(terms, NY), side_by_side(hashes, NY))

        @pl.when(x == 0)
        def _():
            acc_ref[...] = got

        @pl.when(x > 0)
        def _():
            acc_ref[...] += got

        return 0

    lax.fori_loop(0, NX, plane, 0)
    give.wait()


def sketch(basis, rhs, coeffs, rows, signs):
    vm = pl.BlockSpec(memory_space=pltpu.VMEM)
    hbm = pl.BlockSpec(memory_space=pl.ANY)
    return pl.pallas_call(
        sketch_body,
        in_specs=[vm, vm, hbm, hbm, hbm],
        out_specs=(vm, hbm),
        out_shape=(
            jax.ShapeDtypeStruct((TALL, M), f32),
            jax.ShapeDtypeStruct((NX, NY, K, NZ), bf16),
        ),
        scratch_shapes=[
            pltpu.VMEM((NX + 2, NY + 2, K, NZ), f32),
            pltpu.VMEM((NY, TALL, NZ), bf16),
            pltpu.VMEM((NY, M, NZ), bf16),
            pltpu.VMEM((NY, NZ), f32),
            pltpu.VMEM((ROWS, NZ), bf16),
            pltpu.VMEM((TERMS, NX, NY, NZ), f32),
            pltpu.VMEM((NNZ, NX, NY, NZ), jnp.int32),
            pltpu.VMEM((NNZ, NX, NY, NZ), jnp.int32),
            pltpu.VMEM((NX, NY, K, NZ), bf16),
            pltpu.SemaphoreType.DMA((4,)),
        ],
        compiler_params=pltpu.CompilerParams(vmem_limit_bytes=56 << 20),
        name="sketch",
    )(basis, rhs, coeffs, rows, signs)


def planes_body(ids_ref, rows_ref, signs_ref, co_ref, x_first, x_second, y_first, y_second):
    for out, x in ((x_first, ids_ref[2]), (x_second, NX - 1 - ids_ref[2])):
        for j in range(NNZ):
            out[j] = rows_ref[j, x].astype(f32)
            out[NNZ + j] = signs_ref[j, x].astype(f32)
        out[2 * NNZ] = co_ref[1, x]
    for out, y in ((y_first, ids_ref[3]), (y_second, NY - 1 - ids_ref[3])):
        for x in range(NX):
            for j in range(NNZ):
                out[j, x:x + 1, :] = rows_ref[j, x, pl.ds(y, 1), :].astype(f32)
                out[NNZ + j, x:x + 1, :] = signs_ref[j, x, pl.ds(y, 1), :].astype(f32)
            out[2 * NNZ, x:x + 1, :] = co_ref[2, x, pl.ds(y, 1), :]


def planes(ids, rows, signs, coeffs):
    vm = pl.BlockSpec(memory_space=pltpu.VMEM)
    along_x = jax.ShapeDtypeStruct((2 * NNZ + 1, NY, NZ), f32)
    along_y = jax.ShapeDtypeStruct((2 * NNZ + 1, NX, NZ), f32)
    return pl.pallas_call(
        planes_body,
        in_specs=[pl.BlockSpec(memory_space=pltpu.SMEM), vm, vm, vm],
        out_shape=(along_x, along_x, along_y, along_y),
        name="planes",
    )(ids, rows, signs, coeffs)


def edge_body(
    ids_ref, acc_hbm, bxl_ref, bxu_ref, byl_ref, byu_ref, xl_ref, xu_ref, yl_ref, yu_ref,
    own_ref, other_ref, acc, terms, hashes, slots, sem,
):
    fetch = pltpu.make_async_copy(acc_hbm, acc, sem.at[0])
    fetch.start()
    put_slots(slots)

    def one(info, v, y_info, place):
        terms[place] = (-info[2 * NNZ, pl.ds(y_info, 1), :] * v.astype(f32)).astype(bf16)
        put_hash(
            hashes,
            slots,
            place,
            lambda j: info[j, pl.ds(y_info, 1), :],
            lambda j: info[NNZ + j, pl.ds(y_info, 1), :] - 0.5,
        )

    for n, (info, values) in enumerate(((xl_ref, bxl_ref), (xu_ref, bxu_ref))):
        def group(y, _):
            one(info, values[0, y], y, y)
            return 0

        lax.fori_loop(0, NY, group, 0, unroll=2)
        got = nt(side_by_side(terms, NY), side_by_side(hashes, NY))
        if n == 0:
            fetch.wait()
        acc[K:2 * K, :] += got

    def group(x, _):
        one(yl_ref, byl_ref[x, 0], x, x)
        one(yu_ref, byu_ref[x, 0], x, NX + x)
        return 0

    lax.fori_loop(0, NX, group, 0)
    acc[2 * K:3 * K, :] += nt(side_by_side(terms, 2 * NX), side_by_side(hashes, 2 * NX))
    c = ids_ref[0]
    row = lax.broadcasted_iota(jnp.int32, (8, NZ), 0)

    def split(i, _):
        mine = pl.multiple_of(c * 2 * K + i * 16, 16)
        theirs = pl.multiple_of((1 - c) * 2 * K + i * 16, 16)
        for l in range(M // NZ):
            own_ref[i, l * 16:l * 16 + 16, :] = acc[pl.ds(mine, 16), l * NZ:(l + 1) * NZ]
            other_ref[i, l * 16:l * 16 + 16, :] = acc[pl.ds(theirs, 16), l * NZ:(l + 1) * NZ].astype(bf16)
        lane = pl.multiple_of(jnp.minimum(i, M // NZ - 1) * NZ, NZ)
        source = acc[TERMS * K:TERMS * K + 8, pl.ds(lane, NZ)]
        source = jnp.where((row == 0) & (i < M // NZ), source, 0.0)
        own_ref[i, BODY:CHUNK, :] = source
        other_ref[i, BODY:CHUNK, :] = in_three(source)
        return 0

    lax.fori_loop(0, SIDE, split, 0)


def edges(ids, acc, bt, infos):
    vm = pl.BlockSpec(memory_space=pltpu.VMEM)
    return pl.pallas_call(
        edge_body,
        grid_spec=pltpu.PrefetchScalarGridSpec(
        num_scalar_prefetch=1,
        grid=(1,),
        in_specs=[
            pl.BlockSpec(memory_space=pl.ANY),
            pl.BlockSpec((1, NY, K, NZ), lambda i, ids: (ids[2], 0, 0, 0)),
            pl.BlockSpec((1, NY, K, NZ), lambda i, ids: (NX - 1 - ids[2], 0, 0, 0)),
            pl.BlockSpec((NX, 1, K, NZ), lambda i, ids: (0, ids[3], 0, 0)),
            pl.BlockSpec((NX, 1, K, NZ), lambda i, ids: (0, NY - 1 - ids[3], 0, 0)),
            vm,
            vm,
            vm,
            vm,
        ],
        out_specs=(vm, vm),
        scratch_shapes=[
            pltpu.VMEM((TALL, M), f32),
            pltpu.VMEM((NY, K, NZ), bf16),
            pltpu.VMEM((NY, M, NZ), bf16),
            pltpu.VMEM((ROWS, NZ), bf16),
            pltpu.SemaphoreType.DMA((1,)),
        ],
        ),
        out_shape=(
            jax.ShapeDtypeStruct((SIDE, CHUNK, NZ), f32),
            jax.ShapeDtypeStruct((SIDE, CHUNK, NZ), bf16),
        ),
        compiler_params=pltpu.CompilerParams(vmem_limit_bytes=56 << 20),
        name="edges",
    )(ids, acc, bt, bt, bt, bt, *infos)


def merge_body(own_ref, got_ref, out_ref):
    def add(i, _):
        out_ref[i, 0:BODY, :] = (own_ref[i, 0:BODY, :] + got_ref[i, 0:BODY, :].astype(f32)).astype(bf16)
        out_ref[i, BODY:CHUNK, :] = in_three(own_ref[i, BODY:CHUNK, :] + from_three(got_ref[i, BODY:CHUNK, :]))
        return 0

    lax.fori_loop(0, SIDE, add, 0)


def merge(own, got):
    return pl.pallas_call(
        merge_body,
        out_shape=jax.ShapeDtypeStruct((SIDE, CHUNK, NZ), bf16),
        name="merge",
    )(own, got)


def total_of(parts_ref, out_ref, count, copies):
    for at in range(0, BODY, 64):
        total = parts_ref[0, at:at + 64, :].astype(f32)
        for i in range(1, count):
            total = total + parts_ref[i, at:at + 64, :].astype(f32)
        total = total.astype(bf16)
        for i in range(copies):
            out_ref[i, at:at + 64, :] = total
    extra = from_three(parts_ref[0, BODY:CHUNK, :])
    for i in range(1, count):
        extra = extra + from_three(parts_ref[i, BODY:CHUNK, :])
    return extra


def first_body(ids_ref, params_ref, parts_ref, out_ref):
    extra = total_of(parts_ref, out_ref, SIDE, DEEP)
    lane = lax.broadcasted_iota(jnp.int32, (8, NZ), 1)
    row = lax.broadcasted_iota(jnp.int32, (8, NZ), 0)
    extra = jnp.where(row == 0, extra, 0.0)
    for q in range(TERMS):
        extra = jnp.where((row == 1) & (lane == q * DEEP + ids_ref[1]), params_ref[0, q], extra)
    extra = in_three(extra)
    for i in range(DEEP):
        out_ref[i, BODY:CHUNK, :] = extra


def first(ids, params, parts):
    sm = pl.BlockSpec(memory_space=pltpu.SMEM)
    return pl.pallas_call(
        first_body,
        in_specs=[sm, sm, pl.BlockSpec(memory_space=pltpu.VMEM)],
        out_shape=jax.ShapeDtypeStruct((DEEP, CHUNK, NZ), bf16),
        name="first",
    )(ids, params, parts)


def second_body(parts_ref, out_ref):
    extra = in_three(total_of(parts_ref, out_ref, DEEP, SIDE))
    for i in range(SIDE):
        out_ref[i, BODY:CHUNK, :] = extra


def second(parts):
    return pl.pallas_call(
        second_body,
        out_shape=jax.ShapeDtypeStruct((SIDE, CHUNK, NZ), bf16),
        name="second",
    )(parts)


def finish_body(
    ids_ref, own_ref, other_ref, order_ref, bt_hbm, out_hbm,
    st, table, extra, weight, pairs, scale, xs, rs, ps, bt_ref, turned, ready, sems,
):
    fetch = pltpu.make_async_copy(bt_hbm, bt_ref, sems.at[0])
    fetch.start()
    c = ids_ref[0]
    half = TERMS * K // 2

    def place(i, _):
        mine = pl.multiple_of(c * half + i * 16, 16)
        theirs = pl.multiple_of((1 - c) * half + i * 16, 16)
        for l in range(M // NZ):
            st[pl.ds(mine, 16), l * NZ:(l + 1) * NZ] = own_ref[i, l * 16:l * 16 + 16, :]
            st[pl.ds(theirs, 16), l * NZ:(l + 1) * NZ] = other_ref[i, l * 16:l * 16 + 16, :]
        return 0

    lax.fori_loop(0, SIDE, place, 0)
    extra[...] = jnp.zeros((NZ, NZ), f32)
    for ref, h in ((own_ref, c), (other_ref, 1 - c)):
        for i in range(SIDE):
            extra[i:i + 1, :] = from_three(ref[i, BODY:CHUNK, :])[1:2, :]
        columns = jnp.transpose(extra[...])
        for i in range(SIDE):
            at = pl.multiple_of(h * CHIPS + i * DEEP, DEEP)
            for q in range(TERMS):
                weight[q, pl.ds(at, DEEP), :] = jnp.broadcast_to(
                    columns[q * DEEP:(q + 1) * DEEP, i:i + 1], (DEEP, K)
                )
    source = jnp.concatenate([own_ref[i, BODY:CHUNK, :] for i in range(M // NZ)], axis=1)
    gram = nt(st[...], st[...])
    projected = nt(source, st[...])
    projected = projected[0:1, :] + (projected[2:3, :] + projected[4:5, :])
    diagonal = lax.broadcasted_iota(jnp.int32, (K, K), 0) == lax.broadcasted_iota(jnp.int32, (K, K), 1)
    sizes = jnp.zeros((POINTS, K), f32)
    right = jnp.zeros((POINTS, K), f32)
    for q in range(TERMS):
        right = right + weight[q] * projected[:, q * K:(q + 1) * K]
    for n, (q, r) in enumerate(PAIRS):
        block = gram[q * K:(q + 1) * K, r * K:(r + 1) * K]
        if q != r:
            block = block + gram[r * K:(r + 1) * K, q * K:(q + 1) * K]
        top = block.astype(bf16)
        table[0:K, n * K:(n + 1) * K] = top
        table[K:2 * K, n * K:(n + 1) * K] = (block - top.astype(f32)).astype(bf16)
        both = weight[q] * weight[r]
        pairs[n] = both
        sizes = sizes + both * jnp.sum(jnp.where(diagonal, block, 0.0), axis=0, keepdims=True)
    scale[...] = 1.0 / sizes
    z0 = right * scale[...]
    xs[...] = jnp.zeros((POINTS, K), f32)
    rs[...] = right
    ps[...] = z0
    start = jnp.sum(right * z0, axis=1, keepdims=True)
    goal = start * TOL2

    def step(rz):
        whole = ps[...]
        short = whole.astype(bf16)
        p = short.astype(f32)
        images = jnp.dot(jnp.concatenate([short, short], axis=1), table[...], preferred_element_type=f32)
        ap = pairs[0] * images[:, 0:K]
        for n in range(1, len(PAIRS)):
            ap = ap + pairs[n] * images[:, n * K:(n + 1) * K]
        pap = jnp.sum(p * ap, axis=1, keepdims=True)
        alpha = jnp.where(pap > 0.0, rz / pap, 0.0)
        xs[...] += alpha * p
        r = rs[...] - alpha * ap
        rs[...] = r
        z = r * scale[...]
        new = jnp.sum(r * z, axis=1, keepdims=True)
        beta = jnp.where(rz > 0.0, new / rz, 0.0)
        ps[...] = z + beta * whole
        return new

    def rounds(carry):
        n, rz, _ = carry
        rz = step(step(rz))
        return (n + 1, rz, jnp.max(jnp.where(rz > goal, 1.0, 0.0)))

    lax.while_loop(lambda s: (s[0] < MAX_ROUNDS) & (s[2] > 0.5), rounds, (jnp.int32(0), start, f32(1.0)))
    wanted = order_ref[...]
    wanted = (
        ((wanted & 1) << 7)
        + ((wanted >> 6) << 5)
        + (((wanted >> 3) & 3) << 3)
        + (((wanted >> 5) & 1) << 2)
        + ((wanted >> 1) & 3)
    )
    pick = jnp.where(lax.broadcasted_iota(jnp.int32, (POINTS, POINTS), 0) == wanted, 1.0, 0.0).astype(bf16)
    coef = xs[...].astype(bf16)
    picked = lax.dot_general(pick, coef, (((0,), (0,)), ((), ())), preferred_element_type=f32)
    picked = picked.astype(bf16)
    fetch.wait()
    gives = []
    for x in range(NX):
        slot = x % 2
        for y in range(0, NY, 2):
            pair = jnp.concatenate([bt_ref[x, y], bt_ref[x, y + 1]], axis=1)
            got = jnp.dot(picked, pair, preferred_element_type=f32)
            for d in range(2):
                turned[pl.ds(y + d, POINTS, stride=NY), :] = got[:, d * NZ:(d + 1) * NZ]
        if x >= 2:
            gives[x - 2].wait()
        ready[slot] = turned[...].reshape(POINTS, NY, NZ).astype(bf16)
        give = pltpu.make_async_copy(ready.at[slot], out_hbm.at[:, x], sems.at[1 + slot])
        give.start()
        gives.append(give)
    gives[NX - 2].wait()
    gives[NX - 1].wait()


def finish(ids, own, other, order, bt):
    vm = pl.BlockSpec(memory_space=pltpu.VMEM)
    hbm = pl.BlockSpec(memory_space=pl.ANY)
    each = pltpu.VMEM((POINTS, K), f32)
    return pl.pallas_call(
        finish_body,
        in_specs=[pl.BlockSpec(memory_space=pltpu.SMEM), vm, vm, vm, hbm],
        out_specs=hbm,
        out_shape=jax.ShapeDtypeStruct((POINTS, NX, NY, NZ), bf16),
        scratch_shapes=[
            pltpu.VMEM((TERMS * K, M), bf16),
            pltpu.VMEM((2 * K, len(PAIRS) * K), bf16),
            pltpu.VMEM((NZ, NZ), f32),
            pltpu.VMEM((TERMS, POINTS, K), f32),
            pltpu.VMEM((len(PAIRS), POINTS, K), f32),
            each,
            each,
            each,
            each,
            pltpu.VMEM((NX, NY, K, NZ), bf16),
            pltpu.VMEM((POINTS * NY, NZ), f32),
            pltpu.VMEM((2, POINTS, NY, NZ), bf16),
            pltpu.SemaphoreType.DMA((3,)),
        ],
        compiler_params=pltpu.CompilerParams(vmem_limit_bytes=56 << 20),
        name="finish",
    )(ids, own, other, order, bt)


NARROW = ("x", "zl")
WIDE = ("y", "zh", "core")
FACE = ("x", "y")
DEPTH = ("zl", "zh")


def swapped(value, axes, pairs):
    return lax.ppermute(value, axes, pairs + [(j, i) for i, j in pairs])


def per_device(basis, rhs, coeffs, rows, signs, params, order):
    at = [lax.axis_index(name).astype(jnp.int32) for name in ("zl", "zh", "core")]
    zl, zh, core = at
    ids = jnp.stack([core, zl * 4 + zh, (1 - zl) * (NX - 1), (1 - core) * (NY - 1)])
    x_first, x_second, y_first, y_second = planes(ids, rows, signs, coeffs)
    pair = [(0, 1)]
    infos = [
        swapped(x_first, "zl", pair),
        swapped(x_second, NARROW, [(i, i + 1) for i in range(1, 7, 2)]),
        swapped(y_first, "core", pair),
        swapped(y_second, WIDE, [(i, i + 1) for i in range(1, 31, 2)]),
    ]
    acc, bt = sketch(basis, rhs, coeffs, rows, signs)
    own, other = edges(ids, acc, bt, infos)
    parts = merge(own, swapped(other, "core", pair))
    parts = lax.all_to_all(parts, FACE, 0, 0, tiled=True)
    parts = lax.all_to_all(first(ids, params, parts), DEPTH, 0, 0, tiled=True)
    mine = lax.all_to_all(second(parts), FACE, 0, 0, tiled=True)
    theirs = swapped(mine, "core", pair)
    return finish(ids, mine, theirs, order.reshape(1, POINTS), bt)


def solution(mesh):
    fine = Mesh(mesh.devices.reshape(4, 2, 4, 4, 2), ("x", "zl", "y", "zh", "core"))
    cells = P(None, NARROW, WIDE, None)
    in_specs = (
        cells,
        P(NARROW, WIDE, None),
        cells,
        cells,
        cells,
        P(NARROW + WIDE, None),
        P(),
    )
    return jax.shard_map(per_device, mesh=fine, in_specs=in_specs, out_specs=cells, check_vma=False)
```

```python
import jax
import jax.numpy as jnp
from jax import lax
from jax.experimental import pallas as pl
from jax.experimental.pallas import tpu as pltpu
from jax.sharding import Mesh
from jax.sharding import PartitionSpec as P

K = 128
M = 1024
TERMS = 4
NNZ = 4
ROWS = M // NNZ
NX = 4
NY = 16
NZ = 128
CELLS = NY * NZ
TALL = TERMS * K + 16
PART = 256
CHIPS = 128
SIDE = 16
DEEP = 8
BODY = 128
CHUNK = BODY + 8
POINTS = 256
TOL2 = 1e-9
MAX_ROUNDS = 256
PAIRS = tuple((q, r) for q in range(TERMS) for r in range(q, TERMS))

f32 = jnp.float32
bf16 = jnp.bfloat16


def put_hash(hash_ref, slot_ref, y, row_of, sign_of):
    for j in range(NNZ):
        row = jnp.broadcast_to(row_of(j), (16, NZ)).astype(bf16)
        sign = jnp.broadcast_to(sign_of(j), (16, NZ)).astype(bf16)
        for s in range(0, ROWS, 16):
            hash_ref[y, j * ROWS + s:j * ROWS + s + 16, :] = jnp.where(
                slot_ref[s:s + 16, :] == row, sign, jnp.zeros((16, NZ), bf16)
            )


def put_slots(slot_ref):
    slot_ref[...] = lax.broadcasted_iota(jnp.int32, (ROWS, NZ), 0).astype(f32).astype(bf16)


def nt(a, b):
    return lax.dot_general(a, b, (((1,), (1,)), ((), ())), preferred_element_type=f32)


def side_by_side(ref, count):
    return jnp.concatenate([ref[y] for y in range(count)], axis=1)


def turning():
    out = lax.broadcasted_iota(jnp.int32, (16 * NY, 16 * NY), 0)
    src = lax.broadcasted_iota(jnp.int32, (16 * NY, 16 * NY), 1)
    return jnp.where((out // 16 == src % 16) & (out % 16 == src // 16), 1.0, 0.0).astype(bf16)


def in_three(extra):
    high = extra.astype(bf16).astype(f32)
    rest = extra - high
    mid = rest.astype(bf16).astype(f32)
    return (high + pltpu.roll(mid, 2, 0) + pltpu.roll(rest - mid, 4, 0)).astype(bf16)


def from_three(coded):
    coded = coded.astype(f32)
    row = lax.broadcasted_iota(jnp.int32, (8, NZ), 0)
    return jnp.where(row < 2, coded + (pltpu.roll(coded, 6, 0) + pltpu.roll(coded, 4, 0)), 0.0)


def sketch_body(
    basis_hbm, rhs_ref, co_hbm, rows_hbm, signs_hbm, acc_hbm, bt_hbm,
    pad, terms, hashes, terms_b, hashes_b, source_ref, slots, basis_ref, co_ref, rows_ref, signs_ref, bt_ref, acc_ref,
    sems, out_sems,
):
    fetches = [
        pltpu.make_async_copy(src, dst, sems.at[i])
        for i, (src, dst) in enumerate(
            ((basis_hbm, basis_ref), (co_hbm, co_ref), (rows_hbm, rows_ref), (signs_hbm, signs_ref))
        )
    ]
    for fetch in fetches:
        fetch.start()
    put_slots(slots)
    none = jnp.zeros((NY + 2, K, NZ), f32)
    pad[0] = none
    pad[NX + 1] = none
    for x in range(NX):
        pad[x + 1, 0] = jnp.zeros((K, NZ), f32)
        pad[x + 1, NY + 1] = jnp.zeros((K, NZ), f32)
    turn = turning()
    source_ref[...] = rhs_ref[...].astype(f32)
    fetches[0].wait()

    def turned(i, _):
        k = pl.multiple_of(i * 16, 16)
        for x in range(0, NX, 2):
            both = jnp.concatenate(
                [basis_ref[pl.ds(k, 16), x + d].reshape(16 * NY, NZ) for d in range(2)], axis=1
            )
            got = jnp.dot(turn, both, preferred_element_type=f32)
            for d in range(2):
                for y in range(NY):
                    tile = got[y * 16:(y + 1) * 16, d * NZ:(d + 1) * NZ]
                    pad[x + d + 1, y + 1, pl.ds(k, 16), :] = tile
                    bt_ref[x + d, y, pl.ds(k, 16), :] = tile.astype(bf16)
        return 0

    lax.fori_loop(0, K // 16, turned, 0)
    give = pltpu.make_async_copy(bt_ref, bt_hbm, sems.at[4])
    give.start()
    for fetch in fetches[1:]:
        fetch.wait()
    lane = lax.broadcasted_iota(jnp.int32, (1, NZ), 1)
    top = lax.broadcasted_iota(jnp.int32, (16, NZ), 0) == 0

    def build(x, y, terms, hashes):
        c0, c1, c2, c3 = (co_ref[q, x, pl.ds(y, 1), :] for q in range(TERMS))
        low3 = jnp.where(lane == 0, 0.0, c3)
        up3 = jnp.where(lane == NZ - 1, 0.0, c3)
        for k in range(0, K, 16):
            at = slice(k, k + 16)
            v = pad[x + 1, y + 1, at, :]
            v2 = v + v
            along_x = v2 - pad[x, y + 1, at, :] - pad[x + 2, y + 1, at, :]
            along_y = v2 - pad[x + 1, y, at, :] - pad[x + 1, y + 2, at, :]
            t3 = c3 * v2 - low3 * pltpu.roll(v, 1, 1) - up3 * pltpu.roll(v, NZ - 1, 1)
            for q, t in enumerate((c0 * v, c1 * along_x, c2 * along_y, t3)):
                terms[y, q * K + k:q * K + k + 16, :] = t.astype(bf16)
        source = source_ref[x, pl.ds(y, 1), :]
        terms[y, TERMS * K:TALL, :] = jnp.where(top, source, 0.0).astype(bf16)
        put_hash(
            hashes,
            slots,
            y,
            lambda j: rows_ref[j, x, pl.ds(y, 1), :].astype(f32),
            lambda j: signs_ref[j, x, pl.ds(y, 1), :].astype(f32) - 0.5,
        )

    buffers = ((terms, hashes), (terms_b, hashes_b))

    def opening(y, _):
        build(0, y, *buffers[0])
        return 0

    lax.fori_loop(0, NY, opening, 0, unroll=2)
    for x in range(NX):
        t, h = buffers[x % 2]

        def block(i, _):
            cols = pl.multiple_of(i * PART, PART)
            got = nt(
                side_by_side(t, NY),
                jnp.concatenate([h[y, pl.ds(cols, PART), :] for y in range(NY)], axis=1),
            )
            acc_ref[i] = got if x == 0 else acc_ref[i] + got
            if x + 1 < NX:
                for d in range(4):
                    build(x + 1, i * 4 + d, *buffers[(x + 1) % 2])
            else:
                pltpu.make_async_copy(acc_ref.at[i], acc_hbm.at[i], out_sems.at[i]).start()
            return 0

        lax.fori_loop(0, M // PART, block, 0)
    for i in range(M // PART):
        pltpu.make_async_copy(acc_ref.at[i], acc_hbm.at[i], out_sems.at[i]).wait()
    give.wait()


def sketch(basis, rhs, coeffs, rows, signs):
    vm = pl.BlockSpec(memory_space=pltpu.VMEM)
    hbm = pl.BlockSpec(memory_space=pl.ANY)
    return pl.pallas_call(
        sketch_body,
        in_specs=[hbm, vm, hbm, hbm, hbm],
        out_specs=(hbm, hbm),
        out_shape=(
            jax.ShapeDtypeStruct((M // PART, TALL, PART), f32),
            jax.ShapeDtypeStruct((NX, NY, K, NZ), bf16),
        ),
        scratch_shapes=[
            pltpu.VMEM((NX + 2, NY + 2, K, NZ), f32),
            pltpu.VMEM((NY, TALL, NZ), bf16),
            pltpu.VMEM((NY, M, NZ), bf16),
            pltpu.VMEM((NY, TALL, NZ), bf16),
            pltpu.VMEM((NY, M, NZ), bf16),
            pltpu.VMEM((NX, NY, NZ), f32),
            pltpu.VMEM((ROWS, NZ), bf16),
            pltpu.VMEM((K, NX, NY, NZ), bf16),
            pltpu.VMEM((TERMS, NX, NY, NZ), f32),
            pltpu.VMEM((NNZ, NX, NY, NZ), jnp.int32),
            pltpu.VMEM((NNZ, NX, NY, NZ), jnp.int32),
            pltpu.VMEM((NX, NY, K, NZ), bf16),
            pltpu.VMEM((M // PART, TALL, PART), f32),
            pltpu.SemaphoreType.DMA((5,)),
            pltpu.SemaphoreType.DMA((M // PART,)),
        ],
        compiler_params=pltpu.CompilerParams(vmem_limit_bytes=56 << 20),
        name="sketch",
    )(basis, rhs, coeffs, rows, signs)


def planes_body(rows_ref, signs_ref, co_ref, x_first, x_second, y_first, y_second, ids_ref):
    zl, zh, core = (lax.axis_index(name).astype(jnp.int32) for name in ("zl", "zh", "core"))
    plane = (1 - zl) * (NX - 1)
    line = (1 - core) * (NY - 1)
    for n, value in enumerate((core, zl * 4 + zh, plane, line)):
        ids_ref[n] = value
    for out, x in ((x_first, plane), (x_second, NX - 1 - plane)):
        for j in range(NNZ):
            out[j] = rows_ref[j, x].astype(f32)
            out[NNZ + j] = signs_ref[j, x].astype(f32)
        out[2 * NNZ] = co_ref[1, x]
    for out, y in ((y_first, line), (y_second, NY - 1 - line)):
        for x in range(NX):
            for j in range(NNZ):
                out[j, x:x + 1, :] = rows_ref[j, x, pl.ds(y, 1), :].astype(f32)
                out[NNZ + j, x:x + 1, :] = signs_ref[j, x, pl.ds(y, 1), :].astype(f32)
            out[2 * NNZ, x:x + 1, :] = co_ref[2, x, pl.ds(y, 1), :]


def planes(rows, signs, coeffs):
    vm = pl.BlockSpec(memory_space=pltpu.VMEM)
    along_x = jax.ShapeDtypeStruct((2 * NNZ + 1, NY, NZ), f32)
    along_y = jax.ShapeDtypeStruct((2 * NNZ + 1, NX, NZ), f32)
    return pl.pallas_call(
        planes_body,
        in_specs=[vm, vm, vm],
        out_specs=(vm, vm, vm, vm, pl.BlockSpec(memory_space=pltpu.SMEM)),
        out_shape=(along_x, along_x, along_y, along_y, jax.ShapeDtypeStruct((4,), jnp.int32)),
        name="planes",
    )(rows, signs, coeffs)


def edge_body(
    ids_ref, acc_hbm, bxl_ref, bxu_ref, byl_ref, byu_ref, xl_ref, xu_ref, yl_ref, yu_ref,
    own_ref, other_ref, acc, terms, hashes, slots, sem,
):
    fetch = pltpu.make_async_copy(acc_hbm, acc, sem.at[0])
    fetch.start()
    put_slots(slots)

    def one(info, v, y_info, place):
        terms[place] = (-info[2 * NNZ, pl.ds(y_info, 1), :] * v.astype(f32)).astype(bf16)
        put_hash(
            hashes,
            slots,
            place,
            lambda j: info[j, pl.ds(y_info, 1), :],
            lambda j: info[NNZ + j, pl.ds(y_info, 1), :] - 0.5,
        )

    for n, (info, values) in enumerate(((xl_ref, bxl_ref), (xu_ref, bxu_ref))):
        def group(y, _):
            one(info, values[0, y], y, y)
            return 0

        lax.fori_loop(0, NY, group, 0, unroll=2)
        got = nt(side_by_side(terms, NY), side_by_side(hashes, NY))
        if n == 0:
            fetch.wait()
        for n in range(M // PART):
            acc[n, K:2 * K, :] += got[:, n * PART:(n + 1) * PART]

    def group(x, _):
        one(yl_ref, byl_ref[x, 0], x, x)
        one(yu_ref, byu_ref[x, 0], x, NX + x)
        return 0

    lax.fori_loop(0, NX, group, 0)
    got = nt(side_by_side(terms, 2 * NX), side_by_side(hashes, 2 * NX))
    for n in range(M // PART):
        acc[n, 2 * K:3 * K, :] += got[:, n * PART:(n + 1) * PART]
    c = ids_ref[0]
    row = lax.broadcasted_iota(jnp.int32, (8, NZ), 0)

    def split(i, _):
        mine = pl.multiple_of(c * 2 * K + i * 16, 16)
        theirs = pl.multiple_of((1 - c) * 2 * K + i * 16, 16)
        for l in range(M // NZ):
            n, lanes = l // 2, slice((l % 2) * NZ, (l % 2 + 1) * NZ)
            own_ref[i, l * 16:l * 16 + 16, :] = acc[n, pl.ds(mine, 16), lanes]
            other_ref[i, l * 16:l * 16 + 16, :] = acc[n, pl.ds(theirs, 16), lanes].astype(bf16)
        part = jnp.minimum(i, M // NZ - 1)
        source = acc[part // 2, TERMS * K:TERMS * K + 8, pl.ds(pl.multiple_of((part % 2) * NZ, NZ), NZ)]
        source = jnp.where((row == 0) & (i < M // NZ), source, 0.0)
        own_ref[i, BODY:CHUNK, :] = source
        other_ref[i, BODY:CHUNK, :] = in_three(source)
        return 0

    lax.fori_loop(0, SIDE, split, 0)


def edges(ids, acc, bt, infos):
    vm = pl.BlockSpec(memory_space=pltpu.VMEM)
    return pl.pallas_call(
        edge_body,
        grid_spec=pltpu.PrefetchScalarGridSpec(
        num_scalar_prefetch=1,
        grid=(1,),
        in_specs=[
            pl.BlockSpec(memory_space=pl.ANY),
            pl.BlockSpec((1, NY, K, NZ), lambda i, ids: (ids[2], 0, 0, 0)),
            pl.BlockSpec((1, NY, K, NZ), lambda i, ids: (NX - 1 - ids[2], 0, 0, 0)),
            pl.BlockSpec((NX, 1, K, NZ), lambda i, ids: (0, ids[3], 0, 0)),
            pl.BlockSpec((NX, 1, K, NZ), lambda i, ids: (0, NY - 1 - ids[3], 0, 0)),
            vm,
            vm,
            vm,
            vm,
        ],
        out_specs=(vm, vm),
        scratch_shapes=[
            pltpu.VMEM((M // PART, TALL, PART), f32),
            pltpu.VMEM((NY, K, NZ), bf16),
            pltpu.VMEM((NY, M, NZ), bf16),
            pltpu.VMEM((ROWS, NZ), bf16),
            pltpu.SemaphoreType.DMA((1,)),
        ],
        ),
        out_shape=(
            jax.ShapeDtypeStruct((SIDE, CHUNK, NZ), f32),
            jax.ShapeDtypeStruct((SIDE, CHUNK, NZ), bf16),
        ),
        compiler_params=pltpu.CompilerParams(vmem_limit_bytes=56 << 20),
        name="edges",
    )(ids, acc, bt, bt, bt, bt, *infos)


def merge_body(own_hbm, got_hbm, out_hbm, own_ref, got_ref, out_ref, sems):
    size = SIDE // 4
    fetches = [
        [
            pltpu.make_async_copy(src.at[pl.ds(g * size, size)], dst.at[pl.ds(g * size, size)], sems.at[n, g])
            for n, (src, dst) in enumerate(((own_hbm, own_ref), (got_hbm, got_ref)))
        ]
        for g in range(4)
    ]
    for pair in fetches:
        for fetch in pair:
            fetch.start()
    gives = []
    for g in range(4):
        for fetch in fetches[g]:
            fetch.wait()

        def add(i, _):
            out_ref[i, 0:BODY, :] = (own_ref[i, 0:BODY, :] + got_ref[i, 0:BODY, :].astype(f32)).astype(bf16)
            out_ref[i, BODY:CHUNK, :] = in_three(own_ref[i, BODY:CHUNK, :] + from_three(got_ref[i, BODY:CHUNK, :]))
            return 0

        lax.fori_loop(g * size, (g + 1) * size, add, 0)
        part = pl.ds(g * size, size)
        give = pltpu.make_async_copy(out_ref.at[part], out_hbm.at[part], sems.at[2, g])
        give.start()
        gives.append(give)
    for give in gives:
        give.wait()


def merge(own, got):
    hbm = pl.BlockSpec(memory_space=pl.ANY)
    return pl.pallas_call(
        merge_body,
        in_specs=[hbm, hbm],
        out_specs=hbm,
        out_shape=jax.ShapeDtypeStruct((SIDE, CHUNK, NZ), bf16),
        scratch_shapes=[
            pltpu.VMEM((SIDE, CHUNK, NZ), f32),
            pltpu.VMEM((SIDE, CHUNK, NZ), bf16),
            pltpu.VMEM((SIDE, CHUNK, NZ), bf16),
            pltpu.SemaphoreType.DMA((3, 4)),
        ],
        name="merge",
    )(own, got)


def total_of(parts_ref, out_ref, count, copies):
    for at in range(0, BODY, 64):
        total = parts_ref[0, at:at + 64, :].astype(f32)
        for i in range(1, count):
            total = total + parts_ref[i, at:at + 64, :].astype(f32)
        total = total.astype(bf16)
        for i in range(copies):
            out_ref[i, at:at + 64, :] = total
    extra = from_three(parts_ref[0, BODY:CHUNK, :])
    for i in range(1, count):
        extra = extra + from_three(parts_ref[i, BODY:CHUNK, :])
    return extra


def first_body(ids_ref, params_ref, parts_ref, out_ref):
    extra = total_of(parts_ref, out_ref, SIDE, DEEP)
    lane = lax.broadcasted_iota(jnp.int32, (8, NZ), 1)
    row = lax.broadcasted_iota(jnp.int32, (8, NZ), 0)
    extra = jnp.where(row == 0, extra, 0.0)
    for q in range(TERMS):
        extra = jnp.where((row == 1) & (lane == q * DEEP + ids_ref[1]), params_ref[0, q], extra)
    extra = in_three(extra)
    for i in range(DEEP):
        out_ref[i, BODY:CHUNK, :] = extra


def first(ids, params, parts):
    sm = pl.BlockSpec(memory_space=pltpu.SMEM)
    return pl.pallas_call(
        first_body,
        in_specs=[sm, sm, pl.BlockSpec(memory_space=pltpu.VMEM)],
        out_shape=jax.ShapeDtypeStruct((DEEP, CHUNK, NZ), bf16),
        name="first",
    )(ids, params, parts)


def second_body(parts_ref, out_ref):
    extra = in_three(total_of(parts_ref, out_ref, DEEP, SIDE))
    for i in range(SIDE):
        out_ref[i, BODY:CHUNK, :] = extra


def second(parts):
    return pl.pallas_call(
        second_body,
        out_shape=jax.ShapeDtypeStruct((SIDE, CHUNK, NZ), bf16),
        name="second",
    )(parts)


def finish_body(
    ids_ref, own_hbm, other_hbm, order_ref, bt_hbm, out_hbm, own_ref, other_ref,
    st, table, extra, weight, pairs, scale, xs, rs, ps, bt_ref, lines, ready, sems,
):
    halves = [
        pltpu.make_async_copy(own_hbm, own_ref, sems.at[3]),
        pltpu.make_async_copy(other_hbm, other_ref, sems.at[4]),
    ]
    for half in halves:
        half.start()
    fetch = pltpu.make_async_copy(bt_hbm, bt_ref, sems.at[0])
    fetch.start()
    for half in halves:
        half.wait()
    c = ids_ref[0]
    half = TERMS * K // 2

    def place(i, _):
        mine = pl.multiple_of(c * half + i * 16, 16)
        theirs = pl.multiple_of((1 - c) * half + i * 16, 16)
        for l in range(M // NZ):
            st[pl.ds(mine, 16), l * NZ:(l + 1) * NZ] = own_ref[i, l * 16:l * 16 + 16, :]
            st[pl.ds(theirs, 16), l * NZ:(l + 1) * NZ] = other_ref[i, l * 16:l * 16 + 16, :]
        return 0

    lax.fori_loop(0, SIDE, place, 0)
    extra[...] = jnp.zeros((NZ, NZ), f32)
    for ref, h in ((own_ref, c), (other_ref, 1 - c)):
        for i in range(SIDE):
            extra[i:i + 1, :] = from_three(ref[i, BODY:CHUNK, :])[1:2, :]
        columns = jnp.transpose(extra[...])
        for i in range(SIDE):
            at = pl.multiple_of(h * CHIPS + i * DEEP, DEEP)
            for q in range(TERMS):
                weight[q, pl.ds(at, DEEP), :] = jnp.broadcast_to(
                    columns[q * DEEP:(q + 1) * DEEP, i:i + 1], (DEEP, K)
                )
    source = jnp.concatenate([own_ref[i, BODY:CHUNK, :] for i in range(M // NZ)], axis=1)
    gram = nt(st[...], st[...])
    projected = nt(source, st[...])
    projected = projected[0:1, :] + (projected[2:3, :] + projected[4:5, :])
    diagonal = lax.broadcasted_iota(jnp.int32, (K, K), 0) == lax.broadcasted_iota(jnp.int32, (K, K), 1)
    sizes = jnp.zeros((POINTS, K), f32)
    right = jnp.zeros((POINTS, K), f32)
    for q in range(TERMS):
        right = right + weight[q] * projected[:, q * K:(q + 1) * K]
    for n, (q, r) in enumerate(PAIRS):
        block = gram[q * K:(q + 1) * K, r * K:(r + 1) * K]
        if q != r:
            block = block + gram[r * K:(r + 1) * K, q * K:(q + 1) * K]
        top = block.astype(bf16)
        table[0:K, n * K:(n + 1) * K] = top
        table[K:2 * K, n * K:(n + 1) * K] = (block - top.astype(f32)).astype(bf16)
        both = weight[q] * weight[r]
        pairs[n] = both
        sizes = sizes + both * jnp.sum(jnp.where(diagonal, block, 0.0), axis=0, keepdims=True)
    scale[...] = 1.0 / sizes
    z0 = right * scale[...]
    xs[...] = jnp.zeros((POINTS, K), f32)
    rs[...] = right
    ps[...] = z0
    start = jnp.sum(right * z0, axis=1, keepdims=True)
    goal = start * TOL2

    def step(rz):
        whole = ps[...]
        short = whole.astype(bf16)
        p = short.astype(f32)
        images = jnp.dot(jnp.concatenate([short, short], axis=1), table[...], preferred_element_type=f32)
        ap = pairs[0] * images[:, 0:K]
        for n in range(1, len(PAIRS)):
            ap = ap + pairs[n] * images[:, n * K:(n + 1) * K]
        pap = jnp.sum(p * ap, axis=1, keepdims=True)
        alpha = jnp.where(pap > 0.0, rz / pap, 0.0)
        xs[...] += alpha * p
        r = rs[...] - alpha * ap
        rs[...] = r
        z = r * scale[...]
        new = jnp.sum(r * z, axis=1, keepdims=True)
        beta = jnp.where(rz > 0.0, new / rz, 0.0)
        ps[...] = z + beta * whole
        return new

    def rounds(carry):
        n, rz, _ = carry
        rz = step(step(rz))
        return (n + 1, rz, jnp.max(jnp.where(rz > goal, 1.0, 0.0)))

    lax.while_loop(lambda s: (s[0] < MAX_ROUNDS) & (s[2] > 0.5), rounds, (jnp.int32(0), start, f32(1.0)))
    wanted = order_ref[...]
    wanted = (
        ((wanted & 1) << 7)
        + ((wanted >> 6) << 5)
        + (((wanted >> 3) & 3) << 3)
        + (((wanted >> 5) & 1) << 2)
        + ((wanted >> 1) & 3)
    )
    pick = jnp.where(lax.broadcasted_iota(jnp.int32, (POINTS, POINTS), 0) == wanted, 1.0, 0.0).astype(bf16)
    coef = xs[...].astype(bf16)
    picked = lax.dot_general(pick, coef, (((0,), (0,)), ((), ())), preferred_element_type=f32)
    picked = picked.astype(bf16)
    fetch.wait()
    turn = turning()
    gives = []
    for x in range(NX):
        slot = x % 2
        for y in range(0, NY, 2):
            pair = jnp.concatenate([bt_ref[x, y], bt_ref[x, y + 1]], axis=1)
            got = jnp.dot(picked, pair, preferred_element_type=f32).astype(bf16)
            for d in range(2):
                lines[y + d] = got[:, d * NZ:(d + 1) * NZ]
        if x >= 2:
            gives[x - 2].wait()
        for j in range(0, POINTS, 32):
            stack = jnp.concatenate(
                [
                    jnp.concatenate([lines[y, j + d * 16:j + d * 16 + 16, :] for y in range(NY)], axis=0)
                    for d in range(2)
                ],
                axis=1,
            )
            got = jnp.dot(turn, stack, preferred_element_type=f32).astype(bf16)
            for d in range(2):
                ready[slot, j + d * 16:j + d * 16 + 16] = got[:, d * NZ:(d + 1) * NZ].reshape(16, NY, NZ)
        give = pltpu.make_async_copy(ready.at[slot], out_hbm.at[:, x], sems.at[1 + slot])
        give.start()
        gives.append(give)
    gives[NX - 2].wait()
    gives[NX - 1].wait()


def finish(ids, own, other, order, bt):
    vm = pl.BlockSpec(memory_space=pltpu.VMEM)
    hbm = pl.BlockSpec(memory_space=pl.ANY)
    each = pltpu.VMEM((POINTS, K), f32)
    return pl.pallas_call(
        finish_body,
        in_specs=[pl.BlockSpec(memory_space=pltpu.SMEM), hbm, hbm, vm, hbm],
        out_specs=hbm,
        out_shape=jax.ShapeDtypeStruct((POINTS, NX, NY, NZ), bf16),
        scratch_shapes=[
            pltpu.VMEM((SIDE, CHUNK, NZ), bf16),
            pltpu.VMEM((SIDE, CHUNK, NZ), bf16),
            pltpu.VMEM((TERMS * K, M), bf16),
            pltpu.VMEM((2 * K, len(PAIRS) * K), bf16),
            pltpu.VMEM((NZ, NZ), f32),
            pltpu.VMEM((TERMS, POINTS, K), f32),
            pltpu.VMEM((len(PAIRS), POINTS, K), f32),
            each,
            each,
            each,
            each,
            pltpu.VMEM((NX, NY, K, NZ), bf16),
            pltpu.VMEM((NY, POINTS, NZ), bf16),
            pltpu.VMEM((2, POINTS, NY, NZ), bf16),
            pltpu.SemaphoreType.DMA((5,)),
        ],
        compiler_params=pltpu.CompilerParams(vmem_limit_bytes=56 << 20),
        name="finish",
    )(ids, own, other, order, bt)


NARROW = ("x", "zl")
WIDE = ("y", "zh", "core")
FACE = ("x", "y")
DEPTH = ("zl", "zh")


def swapped(value, axes, pairs):
    return lax.ppermute(value, axes, pairs + [(j, i) for i, j in pairs])


def per_device(basis, rhs, coeffs, rows, signs, params, order):
    x_first, x_second, y_first, y_second, ids = planes(rows, signs, coeffs)
    pair = [(0, 1)]
    infos = [
        swapped(x_first, "zl", pair),
        swapped(x_second, NARROW, [(i, i + 1) for i in range(1, 7, 2)]),
        swapped(y_first, "core", pair),
        swapped(y_second, WIDE, [(i, i + 1) for i in range(1, 31, 2)]),
    ]
    acc, bt = sketch(basis, rhs, coeffs, rows, signs)
    own, other = edges(ids, acc, bt, infos)
    parts = merge(own, swapped(other, "core", pair))
    parts = lax.all_to_all(parts, FACE, 0, 0, tiled=True)
    parts = lax.all_to_all(first(ids, params, parts), DEPTH, 0, 0, tiled=True)
    mine = lax.all_to_all(second(parts), FACE, 0, 0, tiled=True)
    theirs = swapped(mine, "core", pair)
    return finish(ids, mine, theirs, order.reshape(1, POINTS), bt)


def solution(mesh):
    fine = Mesh(mesh.devices.reshape(4, 2, 4, 4, 2), ("x", "zl", "y", "zh", "core"))
    cells = P(None, NARROW, WIDE, None)
    in_specs = (
        cells,
        P(NARROW, WIDE, None),
        cells,
        cells,
        cells,
        P(NARROW + WIDE, None),
        P(),
    )
    return jax.shard_map(per_device, mesh=fine, in_specs=in_specs, out_specs=cells, check_vma=False)
```

```python
import jax
import jax.numpy as jnp
from jax import lax
from jax.experimental import pallas as pl
from jax.experimental.pallas import tpu as pltpu
from jax.sharding import Mesh
from jax.sharding import PartitionSpec as P

K = 128
M = 1024
TERMS = 4
NNZ = 4
ROWS = M // NNZ
NX = 4
NY = 16
NZ = 128
CELLS = NY * NZ
TALL = TERMS * K + 16
PART = 256
CHIPS = 128
SIDE = 16
DEEP = 8
BODY = 128
CHUNK = BODY + 8
POINTS = 256
TOL2 = 1e-9
MAX_ROUNDS = 256
PAIRS = tuple((q, r) for q in range(TERMS) for r in range(q, TERMS))

f32 = jnp.float32
bf16 = jnp.bfloat16


def put_hash(hash_ref, slot_ref, y, row_of, sign_of):
    for j in range(NNZ):
        row = jnp.broadcast_to(row_of(j), (16, NZ)).astype(bf16)
        sign = jnp.broadcast_to(sign_of(j), (16, NZ)).astype(bf16)
        for s in range(0, ROWS, 16):
            hash_ref[y, j * ROWS + s:j * ROWS + s + 16, :] = jnp.where(
                slot_ref[s:s + 16, :] == row, sign, jnp.zeros((16, NZ), bf16)
            )


def put_slots(slot_ref):
    slot_ref[...] = lax.broadcasted_iota(jnp.int32, (ROWS, NZ), 0).astype(f32).astype(bf16)


def nt(a, b):
    return lax.dot_general(a, b, (((1,), (1,)), ((), ())), preferred_element_type=f32)


def side_by_side(ref, count):
    return jnp.concatenate([ref[y] for y in range(count)], axis=1)


def turning():
    out = lax.broadcasted_iota(jnp.int32, (16 * NY, 16 * NY), 0)
    src = lax.broadcasted_iota(jnp.int32, (16 * NY, 16 * NY), 1)
    return jnp.where((out // 16 == src % 16) & (out % 16 == src // 16), 1.0, 0.0).astype(bf16)


def in_three(extra):
    high = extra.astype(bf16).astype(f32)
    rest = extra - high
    mid = rest.astype(bf16).astype(f32)
    return (high + pltpu.roll(mid, 2, 0) + pltpu.roll(rest - mid, 4, 0)).astype(bf16)


def from_three(coded):
    coded = coded.astype(f32)
    row = lax.broadcasted_iota(jnp.int32, (8, NZ), 0)
    return jnp.where(row < 2, coded + (pltpu.roll(coded, 6, 0) + pltpu.roll(coded, 4, 0)), 0.0)


def sketch_body(
    basis_hbm, rhs_ref, co_hbm, rows_hbm, signs_hbm, acc_hbm, bt_hbm,
    pad, terms, hashes, terms_b, hashes_b, source_ref, slots, basis_ref, co_ref, rows_ref, signs_ref, bt_ref, acc_ref,
    sems, out_sems, slab_sems,
):
    fetches = [
        pltpu.make_async_copy(src, dst, sems.at[i])
        for i, (src, dst) in enumerate(
            ((co_hbm, co_ref), (rows_hbm, rows_ref), (signs_hbm, signs_ref))
        )
    ]

    def slab(i):
        at = pl.ds(pl.multiple_of(i * 16, 16), 16)
        return pltpu.make_async_copy(basis_hbm.at[at], basis_ref.at[at], slab_sems.at[i])

    for i in range(K // 16):
        slab(i).start()
    for fetch in fetches:
        fetch.start()
    put_slots(slots)
    none = jnp.zeros((NY + 2, K, NZ), f32)
    pad[0] = none
    pad[NX + 1] = none
    for x in range(NX):
        pad[x + 1, 0] = jnp.zeros((K, NZ), f32)
        pad[x + 1, NY + 1] = jnp.zeros((K, NZ), f32)
    turn = turning()
    source_ref[...] = rhs_ref[...].astype(f32)

    def turned(i, _):
        slab(i).wait()
        k = pl.multiple_of(i * 16, 16)
        for x in range(0, NX, 2):
            both = jnp.concatenate(
                [basis_ref[pl.ds(k, 16), x + d].reshape(16 * NY, NZ) for d in range(2)], axis=1
            )
            got = jnp.dot(turn, both, preferred_element_type=f32)
            for d in range(2):
                for y in range(NY):
                    tile = got[y * 16:(y + 1) * 16, d * NZ:(d + 1) * NZ]
                    pad[x + d + 1, y + 1, pl.ds(k, 16), :] = tile
                    bt_ref[x + d, y, pl.ds(k, 16), :] = tile.astype(bf16)
        return 0

    lax.fori_loop(0, K // 16, turned, 0)
    give = pltpu.make_async_copy(bt_ref, bt_hbm, sems.at[4])
    give.start()
    for fetch in fetches:
        fetch.wait()
    lane = lax.broadcasted_iota(jnp.int32, (1, NZ), 1)
    top = lax.broadcasted_iota(jnp.int32, (16, NZ), 0) == 0

    def build(x, y, terms, hashes):
        c0, c1, c2, c3 = (co_ref[q, x, pl.ds(y, 1), :] for q in range(TERMS))
        low3 = jnp.where(lane == 0, 0.0, c3)
        up3 = jnp.where(lane == NZ - 1, 0.0, c3)
        for k in range(0, K, 16):
            at = slice(k, k + 16)
            v = pad[x + 1, y + 1, at, :]
            v2 = v + v
            along_x = v2 - pad[x, y + 1, at, :] - pad[x + 2, y + 1, at, :]
            along_y = v2 - pad[x + 1, y, at, :] - pad[x + 1, y + 2, at, :]
            t3 = c3 * v2 - low3 * pltpu.roll(v, 1, 1) - up3 * pltpu.roll(v, NZ - 1, 1)
            for q, t in enumerate((c0 * v, c1 * along_x, c2 * along_y, t3)):
                terms[y, q * K + k:q * K + k + 16, :] = t.astype(bf16)
        source = source_ref[x, pl.ds(y, 1), :]
        terms[y, TERMS * K:TALL, :] = jnp.where(top, source, 0.0).astype(bf16)
        put_hash(
            hashes,
            slots,
            y,
            lambda j: rows_ref[j, x, pl.ds(y, 1), :].astype(f32),
            lambda j: signs_ref[j, x, pl.ds(y, 1), :].astype(f32) - 0.5,
        )

    buffers = ((terms, hashes), (terms_b, hashes_b))

    def opening(y, _):
        build(0, y, *buffers[0])
        return 0

    lax.fori_loop(0, NY, opening, 0, unroll=2)
    for x in range(NX):
        t, h = buffers[x % 2]

        def block(i, _):
            cols = pl.multiple_of(i * PART, PART)
            got = nt(
                side_by_side(t, NY),
                jnp.concatenate([h[y, pl.ds(cols, PART), :] for y in range(NY)], axis=1),
            )
            acc_ref[i] = got if x == 0 else acc_ref[i] + got
            if x + 1 < NX:
                for d in range(4):
                    build(x + 1, i * 4 + d, *buffers[(x + 1) % 2])
            else:
                pltpu.make_async_copy(acc_ref.at[i], acc_hbm.at[i], out_sems.at[i]).start()
            return 0

        lax.fori_loop(0, M // PART, block, 0)
    for i in range(M // PART):
        pltpu.make_async_copy(acc_ref.at[i], acc_hbm.at[i], out_sems.at[i]).wait()
    give.wait()


def sketch(basis, rhs, coeffs, rows, signs):
    vm = pl.BlockSpec(memory_space=pltpu.VMEM)
    hbm = pl.BlockSpec(memory_space=pl.ANY)
    return pl.pallas_call(
        sketch_body,
        in_specs=[hbm, vm, hbm, hbm, hbm],
        out_specs=(hbm, hbm),
        out_shape=(
            jax.ShapeDtypeStruct((M // PART, TALL, PART), f32),
            jax.ShapeDtypeStruct((NX, NY, K, NZ), bf16),
        ),
        scratch_shapes=[
            pltpu.VMEM((NX + 2, NY + 2, K, NZ), f32),
            pltpu.VMEM((NY, TALL, NZ), bf16),
            pltpu.VMEM((NY, M, NZ), bf16),
            pltpu.VMEM((NY, TALL, NZ), bf16),
            pltpu.VMEM((NY, M, NZ), bf16),
            pltpu.VMEM((NX, NY, NZ), f32),
            pltpu.VMEM((ROWS, NZ), bf16),
            pltpu.VMEM((K, NX, NY, NZ), bf16),
            pltpu.VMEM((TERMS, NX, NY, NZ), f32),
            pltpu.VMEM((NNZ, NX, NY, NZ), jnp.int32),
            pltpu.VMEM((NNZ, NX, NY, NZ), jnp.int32),
            pltpu.VMEM((NX, NY, K, NZ), bf16),
            pltpu.VMEM((M // PART, TALL, PART), f32),
            pltpu.SemaphoreType.DMA((5,)),
            pltpu.SemaphoreType.DMA((M // PART,)),
            pltpu.SemaphoreType.DMA((K // 16,)),
        ],
        compiler_params=pltpu.CompilerParams(vmem_limit_bytes=56 << 20),
        name="sketch",
    )(basis, rhs, coeffs, rows, signs)


def planes_body(rows_ref, signs_ref, co_ref, x_first, x_second, y_first, y_second, ids_ref):
    zl, zh, core = (lax.axis_index(name).astype(jnp.int32) for name in ("zl", "zh", "core"))
    plane = (1 - zl) * (NX - 1)
    line = (1 - core) * (NY - 1)
    for n, value in enumerate((core, zl * 4 + zh, plane, line)):
        ids_ref[n] = value
    for out, x in ((x_first, plane), (x_second, NX - 1 - plane)):
        for j in range(NNZ):
            out[j] = rows_ref[j, x].astype(f32)
            out[NNZ + j] = signs_ref[j, x].astype(f32)
        out[2 * NNZ] = co_ref[1, x]
    for out, y in ((y_first, line), (y_second, NY - 1 - line)):
        for x in range(NX):
            for j in range(NNZ):
                out[j, x:x + 1, :] = rows_ref[j, x, pl.ds(y, 1), :].astype(f32)
                out[NNZ + j, x:x + 1, :] = signs_ref[j, x, pl.ds(y, 1), :].astype(f32)
            out[2 * NNZ, x:x + 1, :] = co_ref[2, x, pl.ds(y, 1), :]


def planes(rows, signs, coeffs):
    vm = pl.BlockSpec(memory_space=pltpu.VMEM)
    along_x = jax.ShapeDtypeStruct((2 * NNZ + 1, NY, NZ), f32)
    along_y = jax.ShapeDtypeStruct((2 * NNZ + 1, NX, NZ), f32)
    return pl.pallas_call(
        planes_body,
        in_specs=[vm, vm, vm],
        out_specs=(vm, vm, vm, vm, pl.BlockSpec(memory_space=pltpu.SMEM)),
        out_shape=(along_x, along_x, along_y, along_y, jax.ShapeDtypeStruct((4,), jnp.int32)),
        name="planes",
    )(rows, signs, coeffs)


def edge_body(
    ids_ref, acc_hbm, bxl_ref, bxu_ref, byl_ref, byu_ref, xl_ref, xu_ref, yl_ref, yu_ref,
    own_ref, other_ref, acc, terms, hashes, slots, sem,
):
    fetch = pltpu.make_async_copy(acc_hbm, acc, sem.at[0])
    fetch.start()
    put_slots(slots)

    def one(info, v, y_info, place):
        terms[place] = (-info[2 * NNZ, pl.ds(y_info, 1), :] * v.astype(f32)).astype(bf16)
        put_hash(
            hashes,
            slots,
            place,
            lambda j: info[j, pl.ds(y_info, 1), :],
            lambda j: info[NNZ + j, pl.ds(y_info, 1), :] - 0.5,
        )

    for n, (info, values) in enumerate(((xl_ref, bxl_ref), (xu_ref, bxu_ref))):
        def group(y, _):
            one(info, values[0, y], y, y)
            return 0

        lax.fori_loop(0, NY, group, 0, unroll=2)
        got = nt(side_by_side(terms, NY), side_by_side(hashes, NY))
        if n == 0:
            fetch.wait()
        for n in range(M // PART):
            acc[n, K:2 * K, :] += got[:, n * PART:(n + 1) * PART]

    def group(x, _):
        one(yl_ref, byl_ref[x, 0], x, x)
        one(yu_ref, byu_ref[x, 0], x, NX + x)
        return 0

    lax.fori_loop(0, NX, group, 0)
    got = nt(side_by_side(terms, 2 * NX), side_by_side(hashes, 2 * NX))
    for n in range(M // PART):
        acc[n, 2 * K:3 * K, :] += got[:, n * PART:(n + 1) * PART]
    c = ids_ref[0]
    row = lax.broadcasted_iota(jnp.int32, (8, NZ), 0)

    def split(i, _):
        mine = pl.multiple_of(c * 2 * K + i * 16, 16)
        theirs = pl.multiple_of((1 - c) * 2 * K + i * 16, 16)
        for l in range(M // NZ):
            n, lanes = l // 2, slice((l % 2) * NZ, (l % 2 + 1) * NZ)
            own_ref[i, l * 16:l * 16 + 16, :] = acc[n, pl.ds(mine, 16), lanes]
            other_ref[i, l * 16:l * 16 + 16, :] = acc[n, pl.ds(theirs, 16), lanes].astype(bf16)
        part = jnp.minimum(i, M // NZ - 1)
        source = acc[part // 2, TERMS * K:TERMS * K + 8, pl.ds(pl.multiple_of((part % 2) * NZ, NZ), NZ)]
        source = jnp.where((row == 0) & (i < M // NZ), source, 0.0)
        own_ref[i, BODY:CHUNK, :] = source
        other_ref[i, BODY:CHUNK, :] = in_three(source)
        return 0

    lax.fori_loop(0, SIDE, split, 0)


def edges(ids, acc, bt, infos):
    vm = pl.BlockSpec(memory_space=pltpu.VMEM)
    return pl.pallas_call(
        edge_body,
        grid_spec=pltpu.PrefetchScalarGridSpec(
        num_scalar_prefetch=1,
        grid=(1,),
        in_specs=[
            pl.BlockSpec(memory_space=pl.ANY),
            pl.BlockSpec((1, NY, K, NZ), lambda i, ids: (ids[2], 0, 0, 0)),
            pl.BlockSpec((1, NY, K, NZ), lambda i, ids: (NX - 1 - ids[2], 0, 0, 0)),
            pl.BlockSpec((NX, 1, K, NZ), lambda i, ids: (0, ids[3], 0, 0)),
            pl.BlockSpec((NX, 1, K, NZ), lambda i, ids: (0, NY - 1 - ids[3], 0, 0)),
            vm,
            vm,
            vm,
            vm,
        ],
        out_specs=(vm, vm),
        scratch_shapes=[
            pltpu.VMEM((M // PART, TALL, PART), f32),
            pltpu.VMEM((NY, K, NZ), bf16),
            pltpu.VMEM((NY, M, NZ), bf16),
            pltpu.VMEM((ROWS, NZ), bf16),
            pltpu.SemaphoreType.DMA((1,)),
        ],
        ),
        out_shape=(
            jax.ShapeDtypeStruct((SIDE, CHUNK, NZ), f32),
            jax.ShapeDtypeStruct((SIDE, CHUNK, NZ), bf16),
        ),
        compiler_params=pltpu.CompilerParams(vmem_limit_bytes=56 << 20),
        name="edges",
    )(ids, acc, bt, bt, bt, bt, *infos)


def merge_body(own_hbm, got_ref, out_hbm, own_ref, out_ref, sems):
    size = SIDE // 4
    fetches = [
        pltpu.make_async_copy(own_hbm.at[pl.ds(g * size, size)], own_ref.at[pl.ds(g * size, size)], sems.at[0, g])
        for g in range(4)
    ]
    for fetch in fetches:
        fetch.start()
    gives = []
    for g in range(4):
        fetches[g].wait()

        def add(i, _):
            out_ref[i, 0:BODY, :] = (own_ref[i, 0:BODY, :] + got_ref[i, 0:BODY, :].astype(f32)).astype(bf16)
            out_ref[i, BODY:CHUNK, :] = in_three(own_ref[i, BODY:CHUNK, :] + from_three(got_ref[i, BODY:CHUNK, :]))
            return 0

        lax.fori_loop(g * size, (g + 1) * size, add, 0)
        part = pl.ds(g * size, size)
        give = pltpu.make_async_copy(out_ref.at[part], out_hbm.at[part], sems.at[1, g])
        give.start()
        gives.append(give)
    for give in gives:
        give.wait()


def merge(own, got):
    hbm = pl.BlockSpec(memory_space=pl.ANY)
    return pl.pallas_call(
        merge_body,
        in_specs=[hbm, pl.BlockSpec(memory_space=pltpu.VMEM)],
        out_specs=hbm,
        out_shape=jax.ShapeDtypeStruct((SIDE, CHUNK, NZ), bf16),
        scratch_shapes=[
            pltpu.VMEM((SIDE, CHUNK, NZ), f32),
            pltpu.VMEM((SIDE, CHUNK, NZ), bf16),
            pltpu.SemaphoreType.DMA((2, 4)),
        ],
        name="merge",
    )(own, got)


def total_of(parts_ref, out_ref, count, copies):
    for at in range(0, BODY, 64):
        total = parts_ref[0, at:at + 64, :].astype(f32)
        for i in range(1, count):
            total = total + parts_ref[i, at:at + 64, :].astype(f32)
        total = total.astype(bf16)
        for i in range(copies):
            out_ref[i, at:at + 64, :] = total
    extra = from_three(parts_ref[0, BODY:CHUNK, :])
    for i in range(1, count):
        extra = extra + from_three(parts_ref[i, BODY:CHUNK, :])
    return extra


def first_body(ids_ref, params_ref, parts_ref, out_ref):
    extra = total_of(parts_ref, out_ref, SIDE, DEEP)
    lane = lax.broadcasted_iota(jnp.int32, (8, NZ), 1)
    row = lax.broadcasted_iota(jnp.int32, (8, NZ), 0)
    extra = jnp.where(row == 0, extra, 0.0)
    for q in range(TERMS):
        extra = jnp.where((row == 1) & (lane == q * DEEP + ids_ref[1]), params_ref[0, q], extra)
    extra = in_three(extra)
    for i in range(DEEP):
        out_ref[i, BODY:CHUNK, :] = extra


def first(ids, params, parts):
    sm = pl.BlockSpec(memory_space=pltpu.SMEM)
    return pl.pallas_call(
        first_body,
        in_specs=[sm, sm, pl.BlockSpec(memory_space=pltpu.VMEM)],
        out_shape=jax.ShapeDtypeStruct((DEEP, CHUNK, NZ), bf16),
        name="first",
    )(ids, params, parts)


def second_body(parts_ref, out_ref):
    extra = in_three(total_of(parts_ref, out_ref, DEEP, SIDE))
    for i in range(SIDE):
        out_ref[i, BODY:CHUNK, :] = extra


def second(parts):
    return pl.pallas_call(
        second_body,
        out_shape=jax.ShapeDtypeStruct((SIDE, CHUNK, NZ), bf16),
        name="second",
    )(parts)


def finish_body(
    ids_ref, own_ref, other_ref, order_ref, bt_hbm, out_hbm,
    st, table, extra, weight, pairs, scale, xs, rs, ps, bt_ref, lines, ready, sems,
):
    fetch = pltpu.make_async_copy(bt_hbm, bt_ref, sems.at[0])
    fetch.start()

    c = ids_ref[0]
    half = TERMS * K // 2

    def place(i, _):
        mine = pl.multiple_of(c * half + i * 16, 16)
        theirs = pl.multiple_of((1 - c) * half + i * 16, 16)
        for l in range(M // NZ):
            st[pl.ds(mine, 16), l * NZ:(l + 1) * NZ] = own_ref[i, l * 16:l * 16 + 16, :]
            st[pl.ds(theirs, 16), l * NZ:(l + 1) * NZ] = other_ref[i, l * 16:l * 16 + 16, :]
        return 0

    lax.fori_loop(0, SIDE, place, 0)
    extra[...] = jnp.zeros((NZ, NZ), f32)
    for ref, h in ((own_ref, c), (other_ref, 1 - c)):
        for i in range(SIDE):
            extra[i:i + 1, :] = from_three(ref[i, BODY:CHUNK, :])[1:2, :]
        columns = jnp.transpose(extra[...])
        for i in range(SIDE):
            at = pl.multiple_of(h * CHIPS + i * DEEP, DEEP)
            for q in range(TERMS):
                weight[q, pl.ds(at, DEEP), :] = jnp.broadcast_to(
                    columns[q * DEEP:(q + 1) * DEEP, i:i + 1], (DEEP, K)
                )
    source = jnp.concatenate([own_ref[i, BODY:CHUNK, :] for i in range(M // NZ)], axis=1)
    gram = nt(st[...], st[...])
    projected = nt(source, st[...])
    projected = projected[0:1, :] + (projected[2:3, :] + projected[4:5, :])
    diagonal = lax.broadcasted_iota(jnp.int32, (K, K), 0) == lax.broadcasted_iota(jnp.int32, (K, K), 1)
    sizes = jnp.zeros((POINTS, K), f32)
    right = jnp.zeros((POINTS, K), f32)
    for q in range(TERMS):
        right = right + weight[q] * projected[:, q * K:(q + 1) * K]
    for n, (q, r) in enumerate(PAIRS):
        block = gram[q * K:(q + 1) * K, r * K:(r + 1) * K]
        if q != r:
            block = block + gram[r * K:(r + 1) * K, q * K:(q + 1) * K]
        top = block.astype(bf16)
        table[0:K, n * K:(n + 1) * K] = top
        table[K:2 * K, n * K:(n + 1) * K] = (block - top.astype(f32)).astype(bf16)
        both = weight[q] * weight[r]
        pairs[n] = both
        sizes = sizes + both * jnp.sum(jnp.where(diagonal, block, 0.0), axis=0, keepdims=True)
    scale[...] = 1.0 / sizes
    z0 = right * scale[...]
    xs[...] = jnp.zeros((POINTS, K), f32)
    rs[...] = right
    ps[...] = z0
    start = jnp.sum(right * z0, axis=1, keepdims=True)
    goal = start * TOL2

    def step(rz):
        whole = ps[...]
        short = whole.astype(bf16)
        p = short.astype(f32)
        images = jnp.dot(jnp.concatenate([short, short], axis=1), table[...], preferred_element_type=f32)
        ap = pairs[0] * images[:, 0:K]
        for n in range(1, len(PAIRS)):
            ap = ap + pairs[n] * images[:, n * K:(n + 1) * K]
        pap = jnp.sum(p * ap, axis=1, keepdims=True)
        alpha = jnp.where(pap > 0.0, rz / pap, 0.0)
        xs[...] += alpha * p
        r = rs[...] - alpha * ap
        rs[...] = r
        z = r * scale[...]
        new = jnp.sum(r * z, axis=1, keepdims=True)
        beta = jnp.where(rz > 0.0, new / rz, 0.0)
        ps[...] = z + beta * whole
        return new

    def rounds(carry):
        n, rz, _ = carry
        rz = step(step(rz))
        return (n + 1, rz, jnp.max(jnp.where(rz > goal, 1.0, 0.0)))

    lax.while_loop(lambda s: (s[0] < MAX_ROUNDS) & (s[2] > 0.5), rounds, (jnp.int32(0), start, f32(1.0)))
    wanted = order_ref[...]
    wanted = (
        ((wanted & 1) << 7)
        + ((wanted >> 6) << 5)
        + (((wanted >> 3) & 3) << 3)
        + (((wanted >> 5) & 1) << 2)
        + ((wanted >> 1) & 3)
    )
    pick = jnp.where(lax.broadcasted_iota(jnp.int32, (POINTS, POINTS), 0) == wanted, 1.0, 0.0).astype(bf16)
    coef = xs[...].astype(bf16)
    picked = lax.dot_general(pick, coef, (((0,), (0,)), ((), ())), preferred_element_type=f32)
    picked = picked.astype(bf16)
    fetch.wait()
    turn = turning()
    gives = []
    for x in range(NX):
        slot = x % 2
        for y in range(0, NY, 2):
            pair = jnp.concatenate([bt_ref[x, y], bt_ref[x, y + 1]], axis=1)
            got = jnp.dot(picked, pair, preferred_element_type=f32).astype(bf16)
            for d in range(2):
                lines[y + d] = got[:, d * NZ:(d + 1) * NZ]
        if x >= 2:
            gives[x - 2].wait()
        for j in range(0, POINTS, 32):
            stack = jnp.concatenate(
                [
                    jnp.concatenate([lines[y, j + d * 16:j + d * 16 + 16, :] for y in range(NY)], axis=0)
                    for d in range(2)
                ],
                axis=1,
            )
            got = jnp.dot(turn, stack, preferred_element_type=f32).astype(bf16)
            for d in range(2):
                ready[slot, j + d * 16:j + d * 16 + 16] = got[:, d * NZ:(d + 1) * NZ].reshape(16, NY, NZ)
        give = pltpu.make_async_copy(ready.at[slot], out_hbm.at[:, x], sems.at[1 + slot])
        give.start()
        gives.append(give)
    gives[NX - 2].wait()
    gives[NX - 1].wait()


def finish(ids, own, other, order, bt):
    vm = pl.BlockSpec(memory_space=pltpu.VMEM)
    hbm = pl.BlockSpec(memory_space=pl.ANY)
    each = pltpu.VMEM((POINTS, K), f32)
    return pl.pallas_call(
        finish_body,
        in_specs=[pl.BlockSpec(memory_space=pltpu.SMEM), vm, vm, vm, hbm],
        out_specs=hbm,
        out_shape=jax.ShapeDtypeStruct((POINTS, NX, NY, NZ), bf16),
        scratch_shapes=[
            pltpu.VMEM((TERMS * K, M), bf16),
            pltpu.VMEM((2 * K, len(PAIRS) * K), bf16),
            pltpu.VMEM((NZ, NZ), f32),
            pltpu.VMEM((TERMS, POINTS, K), f32),
            pltpu.VMEM((len(PAIRS), POINTS, K), f32),
            each,
            each,
            each,
            each,
            pltpu.VMEM((NX, NY, K, NZ), bf16),
            pltpu.VMEM((NY, POINTS, NZ), bf16),
            pltpu.VMEM((2, POINTS, NY, NZ), bf16),
            pltpu.SemaphoreType.DMA((3,)),
        ],
        compiler_params=pltpu.CompilerParams(vmem_limit_bytes=56 << 20),
        name="finish",
    )(ids, own, other, order, bt)


NARROW = ("x", "zl")
WIDE = ("y", "zh", "core")
FACE = ("x", "y")
DEPTH = ("zl", "zh")


def near(value):
    return pltpu.with_memory_space_constraint(value, pltpu.MemorySpace.VMEM)


def swapped(value, axes, pairs):
    return near(lax.ppermute(value, axes, pairs + [(j, i) for i, j in pairs]))


def per_device(basis, rhs, coeffs, rows, signs, params, order):
    x_first, x_second, y_first, y_second, ids = planes(rows, signs, coeffs)
    pair = [(0, 1)]
    infos = [
        swapped(x_first, "zl", pair),
        swapped(x_second, NARROW, [(i, i + 1) for i in range(1, 7, 2)]),
        swapped(y_first, "core", pair),
        swapped(y_second, WIDE, [(i, i + 1) for i in range(1, 31, 2)]),
    ]
    acc, bt = sketch(basis, rhs, coeffs, rows, signs)
    own, other = edges(ids, acc, bt, infos)
    parts = merge(own, swapped(other, "core", pair))
    parts = lax.all_to_all(parts, FACE, 0, 0, tiled=True)
    parts = lax.all_to_all(first(ids, params, parts), DEPTH, 0, 0, tiled=True)
    mine = lax.all_to_all(second(parts), FACE, 0, 0, tiled=True)
    theirs = swapped(mine, "core", pair)
    return finish(ids, near(mine), theirs, order.reshape(1, POINTS), bt)


def solution(mesh):
    fine = Mesh(mesh.devices.reshape(4, 2, 4, 4, 2), ("x", "zl", "y", "zh", "core"))
    cells = P(None, NARROW, WIDE, None)
    in_specs = (
        cells,
        P(NARROW, WIDE, None),
        cells,
        cells,
        cells,
        P(NARROW + WIDE, None),
        P(),
    )
    return jax.shard_map(per_device, mesh=fine, in_specs=in_specs, out_specs=cells, check_vma=False)
```

```python
import jax
import jax.numpy as jnp
from jax import lax
from jax.experimental import pallas as pl
from jax.experimental.pallas import tpu as pltpu
from jax.sharding import Mesh
from jax.sharding import PartitionSpec as P

K = 128
M = 1024
TERMS = 4
NNZ = 4
ROWS = M // NNZ
NX = 4
NY = 16
NZ = 128
CELLS = NY * NZ
TALL = TERMS * K + 16
PART = 256
CHIPS = 128
SIDE = 16
DEEP = 8
BODY = 128
CHUNK = BODY + 8
POINTS = 256
TOL2 = 1e-9
MAX_ROUNDS = 256
PAIRS = tuple((q, r) for q in range(TERMS) for r in range(q, TERMS))

f32 = jnp.float32
bf16 = jnp.bfloat16


def put_hash(hash_ref, slot_ref, y, row_of, sign_of):
    for j in range(NNZ):
        row = jnp.broadcast_to(row_of(j), (16, NZ)).astype(bf16)
        sign = jnp.broadcast_to(sign_of(j), (16, NZ)).astype(bf16)
        for s in range(0, ROWS, 16):
            hash_ref[y, j * ROWS + s:j * ROWS + s + 16, :] = jnp.where(
                slot_ref[s:s + 16, :] == row, sign, jnp.zeros((16, NZ), bf16)
            )


def put_slots(slot_ref):
    slot_ref[...] = lax.broadcasted_iota(jnp.int32, (ROWS, NZ), 0).astype(f32).astype(bf16)


def nt(a, b):
    return lax.dot_general(a, b, (((1,), (1,)), ((), ())), preferred_element_type=f32)


def side_by_side(ref, count):
    return jnp.concatenate([ref[y] for y in range(count)], axis=1)


def turning():
    out = lax.broadcasted_iota(jnp.int32, (16 * NY, 16 * NY), 0)
    src = lax.broadcasted_iota(jnp.int32, (16 * NY, 16 * NY), 1)
    return jnp.where((out // 16 == src % 16) & (out % 16 == src // 16), 1.0, 0.0).astype(bf16)


def in_three(extra):
    high = extra.astype(bf16).astype(f32)
    rest = extra - high
    mid = rest.astype(bf16).astype(f32)
    return (high + pltpu.roll(mid, 2, 0) + pltpu.roll(rest - mid, 4, 0)).astype(bf16)


def from_three(coded):
    coded = coded.astype(f32)
    row = lax.broadcasted_iota(jnp.int32, (8, NZ), 0)
    return jnp.where(row < 2, coded + (pltpu.roll(coded, 6, 0) + pltpu.roll(coded, 4, 0)), 0.0)


def sketch_body(
    basis_hbm, rhs_ref, co_hbm, rows_hbm, signs_hbm, acc_hbm, bt_hbm,
    pad, terms, hashes, terms_b, hashes_b, source_ref, slots, basis_ref, co_ref, rows_ref, signs_ref, bt_ref, acc_ref,
    sems, out_sems, slab_sems,
):
    fetches = [
        pltpu.make_async_copy(src, dst, sems.at[i])
        for i, (src, dst) in enumerate(
            ((co_hbm, co_ref), (rows_hbm, rows_ref), (signs_hbm, signs_ref))
        )
    ]

    def slab(i):
        at = pl.ds(pl.multiple_of(i * 16, 16), 16)
        return pltpu.make_async_copy(basis_hbm.at[at], basis_ref.at[at], slab_sems.at[i])

    for i in range(K // 16):
        slab(i).start()
    for fetch in fetches:
        fetch.start()
    put_slots(slots)
    none = jnp.zeros((NY + 2, K, NZ), f32)
    pad[0] = none
    pad[NX + 1] = none
    for x in range(NX):
        pad[x + 1, 0] = jnp.zeros((K, NZ), f32)
        pad[x + 1, NY + 1] = jnp.zeros((K, NZ), f32)
    turn = turning()
    source_ref[...] = rhs_ref[...].astype(f32)

    def turned(i, _):
        slab(i).wait()
        k = pl.multiple_of(i * 16, 16)
        for x in range(0, NX, 2):
            both = jnp.concatenate(
                [basis_ref[pl.ds(k, 16), x + d].reshape(16 * NY, NZ) for d in range(2)], axis=1
            )
            got = jnp.dot(turn, both, preferred_element_type=f32)
            for d in range(2):
                for y in range(NY):
                    tile = got[y * 16:(y + 1) * 16, d * NZ:(d + 1) * NZ]
                    pad[x + d + 1, y + 1, pl.ds(k, 16), :] = tile
                    bt_ref[x + d, y, pl.ds(k, 16), :] = tile.astype(bf16)
        return 0

    lax.fori_loop(0, K // 16, turned, 0)
    give = pltpu.make_async_copy(bt_ref, bt_hbm, sems.at[4])
    give.start()
    for fetch in fetches:
        fetch.wait()
    lane = lax.broadcasted_iota(jnp.int32, (1, NZ), 1)
    top = lax.broadcasted_iota(jnp.int32, (16, NZ), 0) == 0

    def build(x, y, terms, hashes):
        c0, c1, c2, c3 = (co_ref[q, x, pl.ds(y, 1), :] for q in range(TERMS))
        low3 = jnp.where(lane == 0, 0.0, c3)
        up3 = jnp.where(lane == NZ - 1, 0.0, c3)
        for k in range(0, K, 16):
            at = slice(k, k + 16)
            v = pad[x + 1, y + 1, at, :]
            v2 = v + v
            along_x = v2 - pad[x, y + 1, at, :] - pad[x + 2, y + 1, at, :]
            along_y = v2 - pad[x + 1, y, at, :] - pad[x + 1, y + 2, at, :]
            t3 = c3 * v2 - low3 * pltpu.roll(v, 1, 1) - up3 * pltpu.roll(v, NZ - 1, 1)
            for q, t in enumerate((c0 * v, c1 * along_x, c2 * along_y, t3)):
                terms[y, q * K + k:q * K + k + 16, :] = t.astype(bf16)
        source = source_ref[x, pl.ds(y, 1), :]
        terms[y, TERMS * K:TALL, :] = jnp.where(top, source, 0.0).astype(bf16)
        put_hash(
            hashes,
            slots,
            y,
            lambda j: rows_ref[j, x, pl.ds(y, 1), :].astype(f32),
            lambda j: signs_ref[j, x, pl.ds(y, 1), :].astype(f32) - 0.5,
        )

    buffers = ((terms, hashes), (terms_b, hashes_b))

    def opening(y, _):
        build(0, y, *buffers[0])
        return 0

    lax.fori_loop(0, NY, opening, 0, unroll=2)
    for x in range(NX):
        t, h = buffers[x % 2]

        def block(i, _):
            cols = pl.multiple_of(i * PART, PART)
            got = nt(
                side_by_side(t, NY),
                jnp.concatenate([h[y, pl.ds(cols, PART), :] for y in range(NY)], axis=1),
            )
            acc_ref[i] = got if x == 0 else acc_ref[i] + got
            if x + 1 < NX:
                for d in range(4):
                    build(x + 1, i * 4 + d, *buffers[(x + 1) % 2])
            else:
                pltpu.make_async_copy(acc_ref.at[i], acc_hbm.at[i], out_sems.at[i]).start()
            return 0

        lax.fori_loop(0, M // PART, block, 0)
    for i in range(M // PART):
        pltpu.make_async_copy(acc_ref.at[i], acc_hbm.at[i], out_sems.at[i]).wait()
    give.wait()


def sketch(basis, rhs, coeffs, rows, signs):
    vm = pl.BlockSpec(memory_space=pltpu.VMEM)
    hbm = pl.BlockSpec(memory_space=pl.ANY)
    return pl.pallas_call(
        sketch_body,
        in_specs=[hbm, vm, hbm, hbm, hbm],
        out_specs=(hbm, hbm),
        out_shape=(
            jax.ShapeDtypeStruct((M // PART, TALL, PART), f32),
            jax.ShapeDtypeStruct((NX, NY, K, NZ), bf16),
        ),
        scratch_shapes=[
            pltpu.VMEM((NX + 2, NY + 2, K, NZ), f32),
            pltpu.VMEM((NY, TALL, NZ), bf16),
            pltpu.VMEM((NY, M, NZ), bf16),
            pltpu.VMEM((NY, TALL, NZ), bf16),
            pltpu.VMEM((NY, M, NZ), bf16),
            pltpu.VMEM((NX, NY, NZ), f32),
            pltpu.VMEM((ROWS, NZ), bf16),
            pltpu.VMEM((K, NX, NY, NZ), bf16),
            pltpu.VMEM((TERMS, NX, NY, NZ), f32),
            pltpu.VMEM((NNZ, NX, NY, NZ), jnp.int32),
            pltpu.VMEM((NNZ, NX, NY, NZ), jnp.int32),
            pltpu.VMEM((NX, NY, K, NZ), bf16),
            pltpu.VMEM((M // PART, TALL, PART), f32),
            pltpu.SemaphoreType.DMA((5,)),
            pltpu.SemaphoreType.DMA((M // PART,)),
            pltpu.SemaphoreType.DMA((K // 16,)),
        ],
        compiler_params=pltpu.CompilerParams(vmem_limit_bytes=56 << 20),
        name="sketch",
    )(basis, rhs, coeffs, rows, signs)


def planes_body(rows_ref, signs_ref, co_ref, x_first, x_second, y_first, y_second, ids_ref):
    zl, zh, core = (lax.axis_index(name).astype(jnp.int32) for name in ("zl", "zh", "core"))
    plane = (1 - zl) * (NX - 1)
    line = (1 - core) * (NY - 1)
    for n, value in enumerate((core, zl * 4 + zh, plane, line)):
        ids_ref[n] = value
    for out, x in ((x_first, plane), (x_second, NX - 1 - plane)):
        for j in range(NNZ):
            out[j] = rows_ref[j, x].astype(f32)
            out[NNZ + j] = signs_ref[j, x].astype(f32)
        out[2 * NNZ] = co_ref[1, x]
    for out, y in ((y_first, line), (y_second, NY - 1 - line)):
        for x in range(NX):
            for j in range(NNZ):
                out[j, x:x + 1, :] = rows_ref[j, x, pl.ds(y, 1), :].astype(f32)
                out[NNZ + j, x:x + 1, :] = signs_ref[j, x, pl.ds(y, 1), :].astype(f32)
            out[2 * NNZ, x:x + 1, :] = co_ref[2, x, pl.ds(y, 1), :]


def planes(rows, signs, coeffs):
    vm = pl.BlockSpec(memory_space=pltpu.VMEM)
    along_x = jax.ShapeDtypeStruct((2 * NNZ + 1, NY, NZ), f32)
    along_y = jax.ShapeDtypeStruct((2 * NNZ + 1, NX, NZ), f32)
    return pl.pallas_call(
        planes_body,
        in_specs=[vm, vm, vm],
        out_specs=(vm, vm, vm, vm, pl.BlockSpec(memory_space=pltpu.SMEM)),
        out_shape=(along_x, along_x, along_y, along_y, jax.ShapeDtypeStruct((4,), jnp.int32)),
        name="planes",
    )(rows, signs, coeffs)


def edge_body(
    ids_ref, acc_hbm, bxl_ref, bxu_ref, byl_ref, byu_ref, xl_ref, xu_ref, yl_ref, yu_ref,
    own_ref, other_ref, acc, terms, hashes, slots, sem,
):
    fetch = pltpu.make_async_copy(acc_hbm, acc, sem.at[0])
    fetch.start()
    put_slots(slots)

    def one(info, v, y_info, place):
        terms[place] = (-info[2 * NNZ, pl.ds(y_info, 1), :] * v.astype(f32)).astype(bf16)
        put_hash(
            hashes,
            slots,
            place,
            lambda j: info[j, pl.ds(y_info, 1), :],
            lambda j: info[NNZ + j, pl.ds(y_info, 1), :] - 0.5,
        )

    for n, (info, values) in enumerate(((xl_ref, bxl_ref), (xu_ref, bxu_ref))):
        def group(y, _):
            one(info, values[0, y], y, y)
            return 0

        lax.fori_loop(0, NY, group, 0, unroll=2)
        got = nt(side_by_side(terms, NY), side_by_side(hashes, NY))
        if n == 0:
            fetch.wait()
        for n in range(M // PART):
            acc[n, K:2 * K, :] += got[:, n * PART:(n + 1) * PART]

    def group(x, _):
        one(yl_ref, byl_ref[x, 0], x, x)
        one(yu_ref, byu_ref[x, 0], x, NX + x)
        return 0

    lax.fori_loop(0, NX, group, 0)
    got = nt(side_by_side(terms, 2 * NX), side_by_side(hashes, 2 * NX))
    for n in range(M // PART):
        acc[n, 2 * K:3 * K, :] += got[:, n * PART:(n + 1) * PART]
    c = ids_ref[0]
    row = lax.broadcasted_iota(jnp.int32, (8, NZ), 0)

    def split(i, _):
        mine = pl.multiple_of(c * 2 * K + i * 16, 16)
        theirs = pl.multiple_of((1 - c) * 2 * K + i * 16, 16)
        for l in range(M // NZ):
            n, lanes = l // 2, slice((l % 2) * NZ, (l % 2 + 1) * NZ)
            own_ref[i, l * 16:l * 16 + 16, :] = acc[n, pl.ds(mine, 16), lanes]
            other_ref[i, l * 16:l * 16 + 16, :] = acc[n, pl.ds(theirs, 16), lanes].astype(bf16)
        part = jnp.minimum(i, M // NZ - 1)
        source = acc[part // 2, TERMS * K:TERMS * K + 8, pl.ds(pl.multiple_of((part % 2) * NZ, NZ), NZ)]
        source = jnp.where((row == 0) & (i < M // NZ), source, 0.0)
        own_ref[i, BODY:CHUNK, :] = source
        other_ref[i, BODY:CHUNK, :] = in_three(source)
        return 0

    lax.fori_loop(0, SIDE, split, 0)


def edges(ids, acc, bt, infos):
    vm = pl.BlockSpec(memory_space=pltpu.VMEM)
    return pl.pallas_call(
        edge_body,
        grid_spec=pltpu.PrefetchScalarGridSpec(
        num_scalar_prefetch=1,
        grid=(1,),
        in_specs=[
            pl.BlockSpec(memory_space=pl.ANY),
            pl.BlockSpec((1, NY, K, NZ), lambda i, ids: (ids[2], 0, 0, 0)),
            pl.BlockSpec((1, NY, K, NZ), lambda i, ids: (NX - 1 - ids[2], 0, 0, 0)),
            pl.BlockSpec((NX, 1, K, NZ), lambda i, ids: (0, ids[3], 0, 0)),
            pl.BlockSpec((NX, 1, K, NZ), lambda i, ids: (0, NY - 1 - ids[3], 0, 0)),
            vm,
            vm,
            vm,
            vm,
        ],
        out_specs=(vm, vm),
        scratch_shapes=[
            pltpu.VMEM((M // PART, TALL, PART), f32),
            pltpu.VMEM((NY, K, NZ), bf16),
            pltpu.VMEM((NY, M, NZ), bf16),
            pltpu.VMEM((ROWS, NZ), bf16),
            pltpu.SemaphoreType.DMA((1,)),
        ],
        ),
        out_shape=(
            pltpu.VMEM((SIDE, CHUNK, NZ), f32),
            pltpu.VMEM((SIDE, CHUNK, NZ), bf16),
        ),
        compiler_params=pltpu.CompilerParams(vmem_limit_bytes=56 << 20),
        name="edges",
    )(ids, acc, bt, bt, bt, bt, *infos)


def merge_body(own_ref, got_ref, out_ref):
    def add(i, _):
        out_ref[i, 0:BODY, :] = (own_ref[i, 0:BODY, :] + got_ref[i, 0:BODY, :].astype(f32)).astype(bf16)
        out_ref[i, BODY:CHUNK, :] = in_three(own_ref[i, BODY:CHUNK, :] + from_three(got_ref[i, BODY:CHUNK, :]))
        return 0

    lax.fori_loop(0, SIDE, add, 0)


def merge(own, got):
    vm = pl.BlockSpec(memory_space=pltpu.VMEM)
    return pl.pallas_call(
        merge_body,
        in_specs=[vm, vm],
        out_specs=vm,
        out_shape=pltpu.VMEM((SIDE, CHUNK, NZ), bf16),
        name="merge",
    )(own, got)


def total_of(parts_ref, out_ref, count, copies):
    for at in range(0, BODY, 64):
        total = parts_ref[0, at:at + 64, :].astype(f32)
        for i in range(1, count):
            total = total + parts_ref[i, at:at + 64, :].astype(f32)
        total = total.astype(bf16)
        for i in range(copies):
            out_ref[i, at:at + 64, :] = total
    extra = from_three(parts_ref[0, BODY:CHUNK, :])
    for i in range(1, count):
        extra = extra + from_three(parts_ref[i, BODY:CHUNK, :])
    return extra


def first_body(ids_ref, params_ref, parts_ref, out_ref):
    extra = total_of(parts_ref, out_ref, SIDE, DEEP)
    lane = lax.broadcasted_iota(jnp.int32, (8, NZ), 1)
    row = lax.broadcasted_iota(jnp.int32, (8, NZ), 0)
    extra = jnp.where(row == 0, extra, 0.0)
    for q in range(TERMS):
        extra = jnp.where((row == 1) & (lane == q * DEEP + ids_ref[1]), params_ref[0, q], extra)
    extra = in_three(extra)
    for i in range(DEEP):
        out_ref[i, BODY:CHUNK, :] = extra


def first(ids, params, parts):
    sm = pl.BlockSpec(memory_space=pltpu.SMEM)
    return pl.pallas_call(
        first_body,
        in_specs=[sm, sm, pl.BlockSpec(memory_space=pltpu.VMEM)],
        out_shape=pltpu.VMEM((DEEP, CHUNK, NZ), bf16),
        name="first",
    )(ids, params, parts)


def second_body(parts_ref, out_ref):
    extra = in_three(total_of(parts_ref, out_ref, DEEP, SIDE))
    for i in range(SIDE):
        out_ref[i, BODY:CHUNK, :] = extra


def second(parts):
    return pl.pallas_call(
        second_body,
        in_specs=[pl.BlockSpec(memory_space=pltpu.VMEM)],
        out_shape=pltpu.VMEM((SIDE, CHUNK, NZ), bf16),
        name="second",
    )(parts)


def finish_body(
    ids_ref, own_ref, other_ref, order_ref, bt_hbm, out_hbm,
    st, table, extra, weight, pairs, scale, xs, rs, ps, bt_ref, lines, ready, sems,
):
    fetch = pltpu.make_async_copy(bt_hbm, bt_ref, sems.at[0])
    fetch.start()

    c = ids_ref[0]
    half = TERMS * K // 2

    def place(i, _):
        mine = pl.multiple_of(c * half + i * 16, 16)
        theirs = pl.multiple_of((1 - c) * half + i * 16, 16)
        for l in range(M // NZ):
            st[pl.ds(mine, 16), l * NZ:(l + 1) * NZ] = own_ref[i, l * 16:l * 16 + 16, :]
            st[pl.ds(theirs, 16), l * NZ:(l + 1) * NZ] = other_ref[i, l * 16:l * 16 + 16, :]
        return 0

    lax.fori_loop(0, SIDE, place, 0)
    extra[...] = jnp.zeros((NZ, NZ), f32)
    for ref, h in ((own_ref, c), (other_ref, 1 - c)):
        for i in range(SIDE):
            extra[i:i + 1, :] = from_three(ref[i, BODY:CHUNK, :])[1:2, :]
        columns = jnp.transpose(extra[...])
        for i in range(SIDE):
            at = pl.multiple_of(h * CHIPS + i * DEEP, DEEP)
            for q in range(TERMS):
                weight[q, pl.ds(at, DEEP), :] = jnp.broadcast_to(
                    columns[q * DEEP:(q + 1) * DEEP, i:i + 1], (DEEP, K)
                )
    source = jnp.concatenate([own_ref[i, BODY:CHUNK, :] for i in range(M // NZ)], axis=1)
    gram = nt(st[...], st[...])
    projected = nt(source, st[...])
    projected = projected[0:1, :] + (projected[2:3, :] + projected[4:5, :])
    diagonal = lax.broadcasted_iota(jnp.int32, (K, K), 0) == lax.broadcasted_iota(jnp.int32, (K, K), 1)
    sizes = jnp.zeros((POINTS, K), f32)
    right = jnp.zeros((POINTS, K), f32)
    for q in range(TERMS):
        right = right + weight[q] * projected[:, q * K:(q + 1) * K]
    for n, (q, r) in enumerate(PAIRS):
        block = gram[q * K:(q + 1) * K, r * K:(r + 1) * K]
        if q != r:
            block = block + gram[r * K:(r + 1) * K, q * K:(q + 1) * K]
        top = block.astype(bf16)
        table[0:K, n * K:(n + 1) * K] = top
        table[K:2 * K, n * K:(n + 1) * K] = (block - top.astype(f32)).astype(bf16)
        both = weight[q] * weight[r]
        pairs[n] = both
        sizes = sizes + both * jnp.sum(jnp.where(diagonal, block, 0.0), axis=0, keepdims=True)
    scale[...] = 1.0 / sizes
    z0 = right * scale[...]
    xs[...] = jnp.zeros((POINTS, K), f32)
    rs[...] = right
    ps[...] = z0
    start = jnp.sum(right * z0, axis=1, keepdims=True)
    goal = start * TOL2

    def step(rz):
        whole = ps[...]
        short = whole.astype(bf16)
        p = short.astype(f32)
        images = jnp.dot(jnp.concatenate([short, short], axis=1), table[...], preferred_element_type=f32)
        ap = pairs[0] * images[:, 0:K]
        for n in range(1, len(PAIRS)):
            ap = ap + pairs[n] * images[:, n * K:(n + 1) * K]
        pap = jnp.sum(p * ap, axis=1, keepdims=True)
        alpha = jnp.where(pap > 0.0, rz / pap, 0.0)
        xs[...] += alpha * p
        r = rs[...] - alpha * ap
        rs[...] = r
        z = r * scale[...]
        new = jnp.sum(r * z, axis=1, keepdims=True)
        beta = jnp.where(rz > 0.0, new / rz, 0.0)
        ps[...] = z + beta * whole
        return new

    def rounds(carry):
        n, rz, _ = carry
        rz = step(step(rz))
        return (n + 1, rz, jnp.max(jnp.where(rz > goal, 1.0, 0.0)))

    lax.while_loop(lambda s: (s[0] < MAX_ROUNDS) & (s[2] > 0.5), rounds, (jnp.int32(0), start, f32(1.0)))
    wanted = order_ref[...]
    wanted = (
        ((wanted & 1) << 7)
        + ((wanted >> 6) << 5)
        + (((wanted >> 3) & 3) << 3)
        + (((wanted >> 5) & 1) << 2)
        + ((wanted >> 1) & 3)
    )
    pick = jnp.where(lax.broadcasted_iota(jnp.int32, (POINTS, POINTS), 0) == wanted, 1.0, 0.0).astype(bf16)
    coef = xs[...].astype(bf16)
    picked = lax.dot_general(pick, coef, (((0,), (0,)), ((), ())), preferred_element_type=f32)
    picked = picked.astype(bf16)
    fetch.wait()
    turn = turning()
    gives = []
    for x in range(NX):
        slot = x % 2
        for y in range(0, NY, 2):
            pair = jnp.concatenate([bt_ref[x, y], bt_ref[x, y + 1]], axis=1)
            got = jnp.dot(picked, pair, preferred_element_type=f32).astype(bf16)
            for d in range(2):
                lines[y + d] = got[:, d * NZ:(d + 1) * NZ]
        if x >= 2:
            gives[x - 2].wait()
        for j in range(0, POINTS, 32):
            stack = jnp.concatenate(
                [
                    jnp.concatenate([lines[y, j + d * 16:j + d * 16 + 16, :] for y in range(NY)], axis=0)
                    for d in range(2)
                ],
                axis=1,
            )
            got = jnp.dot(turn, stack, preferred_element_type=f32).astype(bf16)
            for d in range(2):
                ready[slot, j + d * 16:j + d * 16 + 16] = got[:, d * NZ:(d + 1) * NZ].reshape(16, NY, NZ)
        give = pltpu.make_async_copy(ready.at[slot], out_hbm.at[:, x], sems.at[1 + slot])
        give.start()
        gives.append(give)
    gives[NX - 2].wait()
    gives[NX - 1].wait()


def finish(ids, own, other, order, bt):
    vm = pl.BlockSpec(memory_space=pltpu.VMEM)
    hbm = pl.BlockSpec(memory_space=pl.ANY)
    each = pltpu.VMEM((POINTS, K), f32)
    return pl.pallas_call(
        finish_body,
        in_specs=[pl.BlockSpec(memory_space=pltpu.SMEM), vm, vm, vm, hbm],
        out_specs=hbm,
        out_shape=jax.ShapeDtypeStruct((POINTS, NX, NY, NZ), bf16),
        scratch_shapes=[
            pltpu.VMEM((TERMS * K, M), bf16),
            pltpu.VMEM((2 * K, len(PAIRS) * K), bf16),
            pltpu.VMEM((NZ, NZ), f32),
            pltpu.VMEM((TERMS, POINTS, K), f32),
            pltpu.VMEM((len(PAIRS), POINTS, K), f32),
            each,
            each,
            each,
            each,
            pltpu.VMEM((NX, NY, K, NZ), bf16),
            pltpu.VMEM((NY, POINTS, NZ), bf16),
            pltpu.VMEM((2, POINTS, NY, NZ), bf16),
            pltpu.SemaphoreType.DMA((3,)),
        ],
        compiler_params=pltpu.CompilerParams(vmem_limit_bytes=56 << 20),
        name="finish",
    )(ids, own, other, order, bt)


NARROW = ("x", "zl")
WIDE = ("y", "zh", "core")
FACE = ("x", "y")
DEPTH = ("zl", "zh")


def near(value):
    return pltpu.with_memory_space_constraint(value, pltpu.MemorySpace.VMEM)


def swapped(value, axes, pairs):
    return near(lax.ppermute(value, axes, pairs + [(j, i) for i, j in pairs]))


def per_device(basis, rhs, coeffs, rows, signs, params, order):
    x_first, x_second, y_first, y_second, ids = planes(rows, signs, coeffs)
    pair = [(0, 1)]
    infos = [
        swapped(x_first, "zl", pair),
        swapped(x_second, NARROW, [(i, i + 1) for i in range(1, 7, 2)]),
        swapped(y_first, "core", pair),
        swapped(y_second, WIDE, [(i, i + 1) for i in range(1, 31, 2)]),
    ]
    acc, bt = sketch(basis, rhs, coeffs, rows, signs)
    own, other = edges(ids, acc, bt, infos)
    parts = merge(near(own), swapped(other, "core", pair))
    parts = near(lax.all_to_all(parts, FACE, 0, 0, tiled=True))
    parts = near(lax.all_to_all(first(ids, params, parts), DEPTH, 0, 0, tiled=True))
    mine = lax.all_to_all(second(parts), FACE, 0, 0, tiled=True)
    theirs = swapped(mine, "core", pair)
    return finish(ids, near(mine), theirs, order.reshape(1, POINTS), bt)


def solution(mesh):
    fine = Mesh(mesh.devices.reshape(4, 2, 4, 4, 2), ("x", "zl", "y", "zh", "core"))
    cells = P(None, NARROW, WIDE, None)
    in_specs = (
        cells,
        P(NARROW, WIDE, None),
        cells,
        cells,
        cells,
        P(NARROW + WIDE, None),
        P(),
    )
    return jax.shard_map(per_device, mesh=fine, in_specs=in_specs, out_specs=cells, check_vma=False)
```

```python
import jax
import jax.numpy as jnp
from jax import lax
from jax.experimental import pallas as pl
from jax.experimental.pallas import tpu as pltpu
from jax.sharding import Mesh
from jax.sharding import PartitionSpec as P

K = 128
M = 1024
TERMS = 4
NNZ = 4
ROWS = M // NNZ
NX = 4
NY = 16
NZ = 128
CELLS = NY * NZ
TALL = TERMS * K + 16
PART = 256
CHIPS = 128
SIDE = 16
DEEP = 8
BODY = 128
CHUNK = BODY + 8
POINTS = 256
TOL2 = 1e-9
MAX_ROUNDS = 256
PAIRS = tuple((q, r) for q in range(TERMS) for r in range(q, TERMS))

f32 = jnp.float32
bf16 = jnp.bfloat16


def put_hash(hash_ref, slot_ref, y, row_of, sign_of):
    for j in range(NNZ):
        row = jnp.broadcast_to(row_of(j), (16, NZ)).astype(bf16)
        sign = jnp.broadcast_to(sign_of(j), (16, NZ)).astype(bf16)
        for s in range(0, ROWS, 16):
            hash_ref[y, j * ROWS + s:j * ROWS + s + 16, :] = jnp.where(
                slot_ref[s:s + 16, :] == row, sign, jnp.zeros((16, NZ), bf16)
            )


def put_slots(slot_ref):
    slot_ref[...] = lax.broadcasted_iota(jnp.int32, (ROWS, NZ), 0).astype(f32).astype(bf16)


def nt(a, b):
    return lax.dot_general(a, b, (((1,), (1,)), ((), ())), preferred_element_type=f32)


def side_by_side(ref, count):
    return jnp.concatenate([ref[y] for y in range(count)], axis=1)


def turning():
    out = lax.broadcasted_iota(jnp.int32, (16 * NY, 16 * NY), 0)
    src = lax.broadcasted_iota(jnp.int32, (16 * NY, 16 * NY), 1)
    return jnp.where((out // 16 == src % 16) & (out % 16 == src // 16), 1.0, 0.0).astype(bf16)


def in_three(extra):
    high = extra.astype(bf16).astype(f32)
    rest = extra - high
    mid = rest.astype(bf16).astype(f32)
    return (high + pltpu.roll(mid, 2, 0) + pltpu.roll(rest - mid, 4, 0)).astype(bf16)


def from_three(coded):
    coded = coded.astype(f32)
    row = lax.broadcasted_iota(jnp.int32, (8, NZ), 0)
    return jnp.where(row < 2, coded + (pltpu.roll(coded, 6, 0) + pltpu.roll(coded, 4, 0)), 0.0)


def sketch_body(
    basis_hbm, rhs_ref, co_hbm, rows_hbm, signs_hbm, acc_ref, bt_hbm,
    pad, terms, hashes, terms_b, hashes_b, source_ref, slots, basis_ref, co_ref, rows_ref, signs_ref, bt_ref,
    sems, slab_sems,
):
    fetches = [
        pltpu.make_async_copy(src, dst, sems.at[i])
        for i, (src, dst) in enumerate(
            ((co_hbm, co_ref), (rows_hbm, rows_ref), (signs_hbm, signs_ref))
        )
    ]

    def slab(i):
        at = pl.ds(pl.multiple_of(i * 16, 16), 16)
        return pltpu.make_async_copy(basis_hbm.at[at], basis_ref.at[at], slab_sems.at[i])

    for i in range(K // 16):
        slab(i).start()
    for fetch in fetches:
        fetch.start()
    put_slots(slots)
    none = jnp.zeros((NY + 2, K, NZ), f32)
    pad[0] = none
    pad[NX + 1] = none
    for x in range(NX):
        pad[x + 1, 0] = jnp.zeros((K, NZ), f32)
        pad[x + 1, NY + 1] = jnp.zeros((K, NZ), f32)
    turn = turning()
    source_ref[...] = rhs_ref[...].astype(f32)

    def turned(i, _):
        slab(i).wait()
        k = pl.multiple_of(i * 16, 16)
        for x in range(0, NX, 2):
            both = jnp.concatenate(
                [basis_ref[pl.ds(k, 16), x + d].reshape(16 * NY, NZ) for d in range(2)], axis=1
            )
            got = jnp.dot(turn, both, preferred_element_type=f32)
            for d in range(2):
                for y in range(NY):
                    tile = got[y * 16:(y + 1) * 16, d * NZ:(d + 1) * NZ]
                    pad[x + d + 1, y + 1, pl.ds(k, 16), :] = tile
                    bt_ref[x + d, y, pl.ds(k, 16), :] = tile.astype(bf16)
        return 0

    lax.fori_loop(0, K // 16, turned, 0)
    give = pltpu.make_async_copy(bt_ref, bt_hbm, sems.at[4])
    give.start()
    for fetch in fetches:
        fetch.wait()
    lane = lax.broadcasted_iota(jnp.int32, (1, NZ), 1)
    top = lax.broadcasted_iota(jnp.int32, (16, NZ), 0) == 0

    def build(x, y, terms, hashes):
        c0, c1, c2, c3 = (co_ref[q, x, pl.ds(y, 1), :] for q in range(TERMS))
        low3 = jnp.where(lane == 0, 0.0, c3)
        up3 = jnp.where(lane == NZ - 1, 0.0, c3)
        for k in range(0, K, 16):
            at = slice(k, k + 16)
            v = pad[x + 1, y + 1, at, :]
            v2 = v + v
            along_x = v2 - pad[x, y + 1, at, :] - pad[x + 2, y + 1, at, :]
            along_y = v2 - pad[x + 1, y, at, :] - pad[x + 1, y + 2, at, :]
            t3 = c3 * v2 - low3 * pltpu.roll(v, 1, 1) - up3 * pltpu.roll(v, NZ - 1, 1)
            for q, t in enumerate((c0 * v, c1 * along_x, c2 * along_y, t3)):
                terms[y, q * K + k:q * K + k + 16, :] = t.astype(bf16)
        source = source_ref[x, pl.ds(y, 1), :]
        terms[y, TERMS * K:TALL, :] = jnp.where(top, source, 0.0).astype(bf16)
        put_hash(
            hashes,
            slots,
            y,
            lambda j: rows_ref[j, x, pl.ds(y, 1), :].astype(f32),
            lambda j: signs_ref[j, x, pl.ds(y, 1), :].astype(f32) - 0.5,
        )

    buffers = ((terms, hashes), (terms_b, hashes_b))

    def opening(y, _):
        build(0, y, *buffers[0])
        return 0

    lax.fori_loop(0, NY, opening, 0, unroll=2)
    for x in range(NX):
        t, h = buffers[x % 2]

        def block(i, _):
            cols = pl.multiple_of(i * PART, PART)
            got = nt(
                side_by_side(t, NY),
                jnp.concatenate([h[y, pl.ds(cols, PART), :] for y in range(NY)], axis=1),
            )
            acc_ref[i] = got if x == 0 else acc_ref[i] + got
            if x + 1 < NX:
                for d in range(4):
                    build(x + 1, i * 4 + d, *buffers[(x + 1) % 2])
            return 0

        lax.fori_loop(0, M // PART, block, 0)
    give.wait()


def sketch(basis, rhs, coeffs, rows, signs):
    vm = pl.BlockSpec(memory_space=pltpu.VMEM)
    hbm = pl.BlockSpec(memory_space=pl.ANY)
    return pl.pallas_call(
        sketch_body,
        in_specs=[hbm, vm, hbm, hbm, hbm],
        out_specs=(vm, hbm),
        out_shape=(
            pltpu.VMEM((M // PART, TALL, PART), f32),
            jax.ShapeDtypeStruct((NX, NY, K, NZ), bf16),
        ),
        scratch_shapes=[
            pltpu.VMEM((NX + 2, NY + 2, K, NZ), f32),
            pltpu.VMEM((NY, TALL, NZ), bf16),
            pltpu.VMEM((NY, M, NZ), bf16),
            pltpu.VMEM((NY, TALL, NZ), bf16),
            pltpu.VMEM((NY, M, NZ), bf16),
            pltpu.VMEM((NX, NY, NZ), f32),
            pltpu.VMEM((ROWS, NZ), bf16),
            pltpu.VMEM((K, NX, NY, NZ), bf16),
            pltpu.VMEM((TERMS, NX, NY, NZ), f32),
            pltpu.VMEM((NNZ, NX, NY, NZ), jnp.int32),
            pltpu.VMEM((NNZ, NX, NY, NZ), jnp.int32),
            pltpu.VMEM((NX, NY, K, NZ), bf16),
            pltpu.SemaphoreType.DMA((5,)),
            pltpu.SemaphoreType.DMA((K // 16,)),
        ],
        compiler_params=pltpu.CompilerParams(vmem_limit_bytes=56 << 20),
        name="sketch",
    )(basis, rhs, coeffs, rows, signs)


def planes_body(rows_ref, signs_ref, co_ref, x_first, x_second, y_first, y_second, ids_ref):
    zl, zh, core = (lax.axis_index(name).astype(jnp.int32) for name in ("zl", "zh", "core"))
    plane = (1 - zl) * (NX - 1)
    line = (1 - core) * (NY - 1)
    for n, value in enumerate((core, zl * 4 + zh, plane, line)):
        ids_ref[n] = value
    for out, x in ((x_first, plane), (x_second, NX - 1 - plane)):
        for j in range(NNZ):
            out[j] = rows_ref[j, x].astype(f32)
            out[NNZ + j] = signs_ref[j, x].astype(f32)
        out[2 * NNZ] = co_ref[1, x]
    for out, y in ((y_first, line), (y_second, NY - 1 - line)):
        for x in range(NX):
            for j in range(NNZ):
                out[j, x:x + 1, :] = rows_ref[j, x, pl.ds(y, 1), :].astype(f32)
                out[NNZ + j, x:x + 1, :] = signs_ref[j, x, pl.ds(y, 1), :].astype(f32)
            out[2 * NNZ, x:x + 1, :] = co_ref[2, x, pl.ds(y, 1), :]


def planes(rows, signs, coeffs):
    vm = pl.BlockSpec(memory_space=pltpu.VMEM)
    along_x = jax.ShapeDtypeStruct((2 * NNZ + 1, NY, NZ), f32)
    along_y = jax.ShapeDtypeStruct((2 * NNZ + 1, NX, NZ), f32)
    return pl.pallas_call(
        planes_body,
        in_specs=[vm, vm, vm],
        out_specs=(vm, vm, vm, vm, pl.BlockSpec(memory_space=pltpu.SMEM)),
        out_shape=(along_x, along_x, along_y, along_y, jax.ShapeDtypeStruct((4,), jnp.int32)),
        name="planes",
    )(rows, signs, coeffs)


def edge_body(
    ids_ref, acc_in, bxl_ref, bxu_ref, byl_ref, byu_ref, xl_ref, xu_ref, yl_ref, yu_ref,
    own_ref, other_ref, acc, terms, hashes, slots,
):
    put_slots(slots)
    acc[...] = acc_in[...]

    def one(info, v, y_info, place):
        terms[place] = (-info[2 * NNZ, pl.ds(y_info, 1), :] * v.astype(f32)).astype(bf16)
        put_hash(
            hashes,
            slots,
            place,
            lambda j: info[j, pl.ds(y_info, 1), :],
            lambda j: info[NNZ + j, pl.ds(y_info, 1), :] - 0.5,
        )

    for n, (info, values) in enumerate(((xl_ref, bxl_ref), (xu_ref, bxu_ref))):
        def group(y, _):
            one(info, values[0, y], y, y)
            return 0

        lax.fori_loop(0, NY, group, 0, unroll=2)
        got = nt(side_by_side(terms, NY), side_by_side(hashes, NY))
        for n in range(M // PART):
            acc[n, K:2 * K, :] += got[:, n * PART:(n + 1) * PART]

    def group(x, _):
        one(yl_ref, byl_ref[x, 0], x, x)
        one(yu_ref, byu_ref[x, 0], x, NX + x)
        return 0

    lax.fori_loop(0, NX, group, 0)
    got = nt(side_by_side(terms, 2 * NX), side_by_side(hashes, 2 * NX))
    for n in range(M // PART):
        acc[n, 2 * K:3 * K, :] += got[:, n * PART:(n + 1) * PART]
    c = ids_ref[0]
    row = lax.broadcasted_iota(jnp.int32, (8, NZ), 0)

    def split(i, _):
        mine = pl.multiple_of(c * 2 * K + i * 16, 16)
        theirs = pl.multiple_of((1 - c) * 2 * K + i * 16, 16)
        for l in range(M // NZ):
            n, lanes = l // 2, slice((l % 2) * NZ, (l % 2 + 1) * NZ)
            own_ref[i, l * 16:l * 16 + 16, :] = acc[n, pl.ds(mine, 16), lanes]
            other_ref[i, l * 16:l * 16 + 16, :] = acc[n, pl.ds(theirs, 16), lanes].astype(bf16)
        part = jnp.minimum(i, M // NZ - 1)
        source = acc[part // 2, TERMS * K:TERMS * K + 8, pl.ds(pl.multiple_of((part % 2) * NZ, NZ), NZ)]
        source = jnp.where((row == 0) & (i < M // NZ), source, 0.0)
        own_ref[i, BODY:CHUNK, :] = source
        other_ref[i, BODY:CHUNK, :] = in_three(source)
        return 0

    lax.fori_loop(0, SIDE, split, 0)


def edges(ids, acc, bt, infos):
    vm = pl.BlockSpec(memory_space=pltpu.VMEM)
    return pl.pallas_call(
        edge_body,
        grid_spec=pltpu.PrefetchScalarGridSpec(
        num_scalar_prefetch=1,
        grid=(1,),
        in_specs=[
            vm,
            pl.BlockSpec((1, NY, K, NZ), lambda i, ids: (ids[2], 0, 0, 0)),
            pl.BlockSpec((1, NY, K, NZ), lambda i, ids: (NX - 1 - ids[2], 0, 0, 0)),
            pl.BlockSpec((NX, 1, K, NZ), lambda i, ids: (0, ids[3], 0, 0)),
            pl.BlockSpec((NX, 1, K, NZ), lambda i, ids: (0, NY - 1 - ids[3], 0, 0)),
            vm,
            vm,
            vm,
            vm,
        ],
        out_specs=(vm, vm),
        scratch_shapes=[
            pltpu.VMEM((M // PART, TALL, PART), f32),
            pltpu.VMEM((NY, K, NZ), bf16),
            pltpu.VMEM((NY, M, NZ), bf16),
            pltpu.VMEM((ROWS, NZ), bf16),
        ],
        ),
        out_shape=(
            pltpu.VMEM((SIDE, CHUNK, NZ), f32),
            pltpu.VMEM((SIDE, CHUNK, NZ), bf16),
        ),
        compiler_params=pltpu.CompilerParams(vmem_limit_bytes=56 << 20),
        name="edges",
    )(ids, acc, bt, bt, bt, bt, *infos)


def merge_body(own_ref, got_ref, out_ref):
    def add(i, _):
        out_ref[i, 0:BODY, :] = (own_ref[i, 0:BODY, :] + got_ref[i, 0:BODY, :].astype(f32)).astype(bf16)
        out_ref[i, BODY:CHUNK, :] = in_three(own_ref[i, BODY:CHUNK, :] + from_three(got_ref[i, BODY:CHUNK, :]))
        return 0

    lax.fori_loop(0, SIDE, add, 0)


def merge(own, got):
    vm = pl.BlockSpec(memory_space=pltpu.VMEM)
    return pl.pallas_call(
        merge_body,
        in_specs=[vm, vm],
        out_specs=vm,
        out_shape=pltpu.VMEM((SIDE, CHUNK, NZ), bf16),
        name="merge",
    )(own, got)


def total_of(parts_ref, out_ref, count, copies):
    for at in range(0, BODY, 64):
        total = parts_ref[0, at:at + 64, :].astype(f32)
        for i in range(1, count):
            total = total + parts_ref[i, at:at + 64, :].astype(f32)
        total = total.astype(bf16)
        for i in range(copies):
            out_ref[i, at:at + 64, :] = total
    extra = from_three(parts_ref[0, BODY:CHUNK, :])
    for i in range(1, count):
        extra = extra + from_three(parts_ref[i, BODY:CHUNK, :])
    return extra


def first_body(ids_ref, params_ref, parts_ref, out_ref):
    extra = total_of(parts_ref, out_ref, SIDE, DEEP)
    lane = lax.broadcasted_iota(jnp.int32, (8, NZ), 1)
    row = lax.broadcasted_iota(jnp.int32, (8, NZ), 0)
    extra = jnp.where(row == 0, extra, 0.0)
    for q in range(TERMS):
        extra = jnp.where((row == 1) & (lane == q * DEEP + ids_ref[1]), params_ref[0, q], extra)
    extra = in_three(extra)
    for i in range(DEEP):
        out_ref[i, BODY:CHUNK, :] = extra


def first(ids, params, parts):
    sm = pl.BlockSpec(memory_space=pltpu.SMEM)
    return pl.pallas_call(
        first_body,
        in_specs=[sm, sm, pl.BlockSpec(memory_space=pltpu.VMEM)],
        out_shape=pltpu.VMEM((DEEP, CHUNK, NZ), bf16),
        name="first",
    )(ids, params, parts)


def second_body(parts_ref, out_ref):
    extra = in_three(total_of(parts_ref, out_ref, DEEP, SIDE))
    for i in range(SIDE):
        out_ref[i, BODY:CHUNK, :] = extra


def second(parts):
    return pl.pallas_call(
        second_body,
        in_specs=[pl.BlockSpec(memory_space=pltpu.VMEM)],
        out_shape=pltpu.VMEM((SIDE, CHUNK, NZ), bf16),
        name="second",
    )(parts)


def finish_body(
    ids_ref, own_ref, other_ref, order_ref, bt_hbm, out_hbm,
    st, table, extra, weight, pairs, scale, xs, rs, ps, bt_ref, lines, ready, sems,
):
    fetch = pltpu.make_async_copy(bt_hbm, bt_ref, sems.at[0])
    fetch.start()

    c = ids_ref[0]
    half = TERMS * K // 2

    def place(i, _):
        mine = pl.multiple_of(c * half + i * 16, 16)
        theirs = pl.multiple_of((1 - c) * half + i * 16, 16)
        for l in range(M // NZ):
            st[pl.ds(mine, 16), l * NZ:(l + 1) * NZ] = own_ref[i, l * 16:l * 16 + 16, :]
            st[pl.ds(theirs, 16), l * NZ:(l + 1) * NZ] = other_ref[i, l * 16:l * 16 + 16, :]
        return 0

    lax.fori_loop(0, SIDE, place, 0)
    extra[...] = jnp.zeros((NZ, NZ), f32)
    for ref, h in ((own_ref, c), (other_ref, 1 - c)):
        for i in range(SIDE):
            extra[i:i + 1, :] = from_three(ref[i, BODY:CHUNK, :])[1:2, :]
        columns = jnp.transpose(extra[...])
        for i in range(SIDE):
            at = pl.multiple_of(h * CHIPS + i * DEEP, DEEP)
            for q in range(TERMS):
                weight[q, pl.ds(at, DEEP), :] = jnp.broadcast_to(
                    columns[q * DEEP:(q + 1) * DEEP, i:i + 1], (DEEP, K)
                )
    source = jnp.concatenate([own_ref[i, BODY:CHUNK, :] for i in range(M // NZ)], axis=1)
    gram = nt(st[...], st[...])
    projected = nt(source, st[...])
    projected = projected[0:1, :] + (projected[2:3, :] + projected[4:5, :])
    diagonal = lax.broadcasted_iota(jnp.int32, (K, K), 0) == lax.broadcasted_iota(jnp.int32, (K, K), 1)
    sizes = jnp.zeros((POINTS, K), f32)
    right = jnp.zeros((POINTS, K), f32)
    for q in range(TERMS):
        right = right + weight[q] * projected[:, q * K:(q + 1) * K]
    for n, (q, r) in enumerate(PAIRS):
        block = gram[q * K:(q + 1) * K, r * K:(r + 1) * K]
        if q != r:
            block = block + gram[r * K:(r + 1) * K, q * K:(q + 1) * K]
        top = block.astype(bf16)
        table[0:K, n * K:(n + 1) * K] = top
        table[K:2 * K, n * K:(n + 1) * K] = (block - top.astype(f32)).astype(bf16)
        both = weight[q] * weight[r]
        pairs[n] = both
        sizes = sizes + both * jnp.sum(jnp.where(diagonal, block, 0.0), axis=0, keepdims=True)
    scale[...] = 1.0 / sizes
    z0 = right * scale[...]
    xs[...] = jnp.zeros((POINTS, K), f32)
    rs[...] = right
    ps[...] = z0
    start = jnp.sum(right * z0, axis=1, keepdims=True)
    goal = start * TOL2

    def step(rz):
        whole = ps[...]
        short = whole.astype(bf16)
        p = short.astype(f32)
        images = jnp.dot(jnp.concatenate([short, short], axis=1), table[...], preferred_element_type=f32)
        ap = pairs[0] * images[:, 0:K]
        for n in range(1, len(PAIRS)):
            ap = ap + pairs[n] * images[:, n * K:(n + 1) * K]
        pap = jnp.sum(p * ap, axis=1, keepdims=True)
        alpha = jnp.where(pap > 0.0, rz / pap, 0.0)
        xs[...] += alpha * p
        r = rs[...] - alpha * ap
        rs[...] = r
        z = r * scale[...]
        new = jnp.sum(r * z, axis=1, keepdims=True)
        beta = jnp.where(rz > 0.0, new / rz, 0.0)
        ps[...] = z + beta * whole
        return new

    def rounds(carry):
        n, rz, _ = carry
        rz = step(step(rz))
        return (n + 1, rz, jnp.max(jnp.where(rz > goal, 1.0, 0.0)))

    lax.while_loop(lambda s: (s[0] < MAX_ROUNDS) & (s[2] > 0.5), rounds, (jnp.int32(0), start, f32(1.0)))
    wanted = order_ref[...]
    wanted = (
        ((wanted & 1) << 7)
        + ((wanted >> 6) << 5)
        + (((wanted >> 3) & 3) << 3)
        + (((wanted >> 5) & 1) << 2)
        + ((wanted >> 1) & 3)
    )
    pick = jnp.where(lax.broadcasted_iota(jnp.int32, (POINTS, POINTS), 0) == wanted, 1.0, 0.0).astype(bf16)
    coef = xs[...].astype(bf16)
    picked = lax.dot_general(pick, coef, (((0,), (0,)), ((), ())), preferred_element_type=f32)
    picked = picked.astype(bf16)
    fetch.wait()
    turn = turning()
    gives = []
    for x in range(NX):
        slot = x % 2
        for y in range(0, NY, 2):
            pair = jnp.concatenate([bt_ref[x, y], bt_ref[x, y + 1]], axis=1)
            got = jnp.dot(picked, pair, preferred_element_type=f32).astype(bf16)
            for d in range(2):
                lines[y + d] = got[:, d * NZ:(d + 1) * NZ]
        if x >= 2:
            gives[x - 2].wait()
        for j in range(0, POINTS, 32):
            stack = jnp.concatenate(
                [
                    jnp.concatenate([lines[y, j + d * 16:j + d * 16 + 16, :] for y in range(NY)], axis=0)
                    for d in range(2)
                ],
                axis=1,
            )
            got = jnp.dot(turn, stack, preferred_element_type=f32).astype(bf16)
            for d in range(2):
                ready[slot, j + d * 16:j + d * 16 + 16] = got[:, d * NZ:(d + 1) * NZ].reshape(16, NY, NZ)
        give = pltpu.make_async_copy(ready.at[slot], out_hbm.at[:, x], sems.at[1 + slot])
        give.start()
        gives.append(give)
    gives[NX - 2].wait()
    gives[NX - 1].wait()


def finish(ids, own, other, order, bt):
    vm = pl.BlockSpec(memory_space=pltpu.VMEM)
    hbm = pl.BlockSpec(memory_space=pl.ANY)
    each = pltpu.VMEM((POINTS, K), f32)
    return pl.pallas_call(
        finish_body,
        in_specs=[pl.BlockSpec(memory_space=pltpu.SMEM), vm, vm, vm, hbm],
        out_specs=hbm,
        out_shape=jax.ShapeDtypeStruct((POINTS, NX, NY, NZ), bf16),
        scratch_shapes=[
            pltpu.VMEM((TERMS * K, M), bf16),
            pltpu.VMEM((2 * K, len(PAIRS) * K), bf16),
            pltpu.VMEM((NZ, NZ), f32),
            pltpu.VMEM((TERMS, POINTS, K), f32),
            pltpu.VMEM((len(PAIRS), POINTS, K), f32),
            each,
            each,
            each,
            each,
            pltpu.VMEM((NX, NY, K, NZ), bf16),
            pltpu.VMEM((NY, POINTS, NZ), bf16),
            pltpu.VMEM((2, POINTS, NY, NZ), bf16),
            pltpu.SemaphoreType.DMA((3,)),
        ],
        compiler_params=pltpu.CompilerParams(vmem_limit_bytes=56 << 20),
        name="finish",
    )(ids, own, other, order, bt)


NARROW = ("x", "zl")
WIDE = ("y", "zh", "core")
FACE = ("x", "y")
DEPTH = ("zl", "zh")


def near(value):
    return pltpu.with_memory_space_constraint(value, pltpu.MemorySpace.VMEM)


def swapped(value, axes, pairs):
    return near(lax.ppermute(value, axes, pairs + [(j, i) for i, j in pairs]))


def per_device(basis, rhs, coeffs, rows, signs, params, order):
    x_first, x_second, y_first, y_second, ids = planes(rows, signs, coeffs)
    pair = [(0, 1)]
    infos = [
        swapped(x_first, "zl", pair),
        swapped(x_second, NARROW, [(i, i + 1) for i in range(1, 7, 2)]),
        swapped(y_first, "core", pair),
        swapped(y_second, WIDE, [(i, i + 1) for i in range(1, 31, 2)]),
    ]
    acc, bt = sketch(basis, rhs, coeffs, rows, signs)
    own, other = edges(ids, near(acc), bt, infos)
    parts = merge(near(own), swapped(other, "core", pair))
    parts = near(lax.all_to_all(parts, FACE, 0, 0, tiled=True))
    parts = near(lax.all_to_all(first(ids, params, parts), DEPTH, 0, 0, tiled=True))
    mine = lax.all_to_all(second(parts), FACE, 0, 0, tiled=True)
    theirs = swapped(mine, "core", pair)
    return finish(ids, near(mine), theirs, order.reshape(1, POINTS), bt)


def solution(mesh):
    fine = Mesh(mesh.devices.reshape(4, 2, 4, 4, 2), ("x", "zl", "y", "zh", "core"))
    cells = P(None, NARROW, WIDE, None)
    in_specs = (
        cells,
        P(NARROW, WIDE, None),
        cells,
        cells,
        cells,
        P(NARROW + WIDE, None),
        P(),
    )
    return jax.shard_map(per_device, mesh=fine, in_specs=in_specs, out_specs=cells, check_vma=False)
```
